768 devices in a mesh: tile: 32 (over x_hi, y, core), trc: 24 (over x_lo, z).
Axes of the slice: x: 4 (x_hi: 2, x_lo: 2; x = x_hi * 2 + x_lo), y: 8, z: 12, core: 2. Of those that a mesh axis runs over, the one named last changes fastest.
Arguments:
- tracers: float32 [96, 8, 256, 128], P('trc', None, 'tile'), may hold values from -6 to 6
- flux_pool: float32 [24, 2, 3, 8, 256, 128], P('trc', None, None, None, 'tile'), may hold values from -0.45 to 0.45
- mass_pool: float32 [24, 2, 8, 256, 128], P('trc', None, None, 'tile'), may hold values from 1 to 2
- owner: int32 [2, 32], P(None, 'tile'), may hold values from 0 to 23
- conv_cols: int32 [32, 256], P('tile'), may hold values from 0 to 1023, as said below
- conv_steps: int32 [32, 256], P('tile'), may hold values from 1 to 3
- conv_rate: float32 [32, 7, 256], P('tile'), may hold values from 0.05 to 0.5
Outputs:
- advected: float32 [96, 8, 256, 128], P('trc', None, 'tile')
The draws below stay inside these ranges and needn't reach their ends.
Inputs may be any that keep to these rules, and one draw needn't show every extreme that they name: `conv_cols`: the 256 columns listed for one tile are all different.
All inputs are finite; a program needn't handle non-finite values.
Results may differ from the reference program's by a relative error of at most 0.0003.
Values sent between devices are 32-bit elements; how exact they have to be, the bound alone decides.
No kernel may reach another device: no remote copies, remote signals or barrier semaphores. Data moves between devices by JAX's collectives and lax.ppermute only.
A program may use at most 32 MiB of HBM per device.

```python
import math
import jax
import jax.numpy as jnp
from jax import lax

CX = 8
NY = 128
NZ = 8
STEPS = 2
TRACERS = 96
NX = 256
CONV = 256
N_TILE = 32
N_TRC = 24


def draw_conv_cols(key, part):
    column_total = CX * NY
    keys_all = jax.random.split(key, N_TILE)
    orders = jax.vmap(lambda single_key: jax.random.permutation(single_key, column_total))(keys_all)[:, :CONV]
    leading = orders[:, 0]
    tile_ids = jnp.arange(N_TILE)
    offsets = jnp.where(tile_ids == 0, column_total - 1 - leading, jnp.where(tile_ids == 1, -leading, 0))
    return ((orders + offsets[:, None]) % column_total).astype(jnp.int32)


def draw_conv_steps(key, part):
    heaviness = jax.random.randint(jax.random.fold_in(key, 1), (N_TILE, 1), 0, 3)
    raw_draw = jax.random.randint(jax.random.fold_in(key, 2), (N_TILE, CONV), 0, 3)
    counts = 1 + jnp.minimum(raw_draw, heaviness)
    counts = counts.at[0, 0].set(3).at[0, 1].set(1)
    return counts.astype(jnp.int32)


def plant(array, stream_key, least, largest):
    longest = array.shape.index(max(array.shape))
    spots = []
    for shift in (0, 1):
        where = [jax.random.randint(jax.random.fold_in(stream_key, axis), (), 0, length) for axis, length in enumerate(array.shape)]
        where[longest] = (where[longest] + shift) % array.shape[longest]
        spots.append(tuple(where))
    return array.at[spots[0]].set(least).at[spots[1]].set(largest)


def level_of(stream_key, dims, pieces, low, top_value):
    loudness = 1.0
    for axis_at, parts in pieces:
        heights = jax.random.uniform(jax.random.fold_in(jax.random.fold_in(stream_key, 6), axis_at), (parts,), jnp.float32, low / len(pieces), top_value / len(pieces))
        loudness = loudness * jnp.repeat(jnp.exp(heights), dims[axis_at] // parts).reshape((-1,) + (1,) * (len(dims) - 1 - axis_at))
    return loudness


def noise(own_key, extent, width, reach, cuts=(), dtype=jnp.bfloat16):
    values = jax.random.normal(own_key, extent, jnp.float32) * width
    if len(cuts) > 0:
        values = level_of(own_key, extent, cuts, -0.22, 0.18) * values
    return jnp.clip(values, min=-reach, max=reach).astype(dtype)


def setup_inputs(seed: int = 0) -> dict:
    streams_of = jax.random.split(jax.random.key(seed), 8)
    tracers = noise(streams_of[0], (TRACERS, NZ, NX, NY), 1.0, 6.0, ((0, 24), (2, 32)), jnp.float32)
    flux_pool = jnp.clip(jax.random.uniform(streams_of[1], (N_TRC, STEPS, 3, NZ, NX, NY), jnp.float32, -0.45, 0.45) * level_of(streams_of[1], (N_TRC, STEPS, 3, NZ, NX, NY), ((0, 24), (4, 32)), -0.4, 0.0), -0.45, 0.45)
    mass_pool = jnp.clip(1.0 + 1.0 * jax.random.uniform(streams_of[2], (N_TRC, STEPS, NZ, NX, NY), jnp.float32) ** level_of(streams_of[2], (N_TRC, STEPS, NZ, NX, NY), ((0, 24), (3, 32)), -0.2, 0.2), 1.0, 2.0)
    owner = plant(jax.random.randint(streams_of[3], (STEPS, N_TILE), 0, N_TRC), jax.random.fold_in(streams_of[3], 1), 0, N_TRC - 1).astype(jnp.int32)
    conv_cols = draw_conv_cols(jax.random.fold_in(streams_of[7], 71), 0)
    conv_steps = draw_conv_steps(jax.random.fold_in(streams_of[7], 71), 0)
    conv_rate = jnp.clip(jnp.exp(math.log(0.5) - 2.3025851 * jax.random.uniform(streams_of[6], (N_TILE, NZ - 1, CONV), jnp.float32) ** level_of(streams_of[6], (N_TILE, NZ - 1, CONV), ((0, 32),), -0.2, 0.2)), 0.05, 0.5)
    return dict(tracers=tracers, flux_pool=flux_pool, mass_pool=mass_pool, owner=owner, conv_cols=conv_cols, conv_steps=conv_steps, conv_rate=conv_rate)


def slab(values_in, first_index, how_many, along):
    position = along % values_in.ndim
    return lax.slice_in_dim(values_in, first_index, first_index + how_many, axis=position)


def pad_axis(values_in, along, pad_low, pad_high, pad_mode):
    widths = [(0, 0)] * values_in.ndim
    widths[along % values_in.ndim] = (pad_low, pad_high)
    return jnp.pad(values_in, widths, mode=pad_mode)


def closed_faces(face_flux, along):
    position = along % face_flux.ndim
    face_count = face_flux.shape[position]
    dims_shape = [1] * face_flux.ndim
    dims_shape[position] = face_count
    kept_mask = (jnp.arange(face_count) < face_count - 1).reshape(dims_shape)
    return jnp.where(kept_mask, face_flux, 0.0)


def parabola_sweep(padded, mass_pad, face_flux, along, length):
    count_edges = length + 3
    outer_left = slab(padded, 0, count_edges, along)
    inner_left = slab(padded, 1, count_edges, along)
    inner_right = slab(padded, 2, count_edges, along)
    outer_right = slab(padded, 3, count_edges, along)
    edge_values = (7.0 / 12.0) * (inner_left + inner_right) - (1.0 / 12.0) * (outer_left + outer_right)
    edge_values = jnp.clip(edge_values, jnp.minimum(inner_left, inner_right), jnp.maximum(inner_left, inner_right))
    count_cells = length + 2
    centre = slab(padded, 2, count_cells, along)
    left_edge = slab(edge_values, 0, count_cells, along)
    right_edge = slab(edge_values, 1, count_cells, along)
    extremum = (right_edge - centre) * (centre - left_edge) <= 0.0
    left_edge = jnp.where(extremum, centre, left_edge)
    right_edge = jnp.where(extremum, centre, right_edge)
    edge_jump = right_edge - left_edge
    curvature = 6.0 * (centre - 0.5 * (left_edge + right_edge))
    new_left = jnp.where(edge_jump * curvature > edge_jump * edge_jump, 3.0 * centre - 2.0 * right_edge, left_edge)
    new_right = jnp.where(-edge_jump * edge_jump > edge_jump * curvature, 3.0 * centre - 2.0 * left_edge, right_edge)
    edge_jump = new_right - new_left
    curvature = 6.0 * (centre - 0.5 * (new_left + new_right))
    face_count = length + 1
    upwind_mass = slab(mass_pad, 0, face_count, along)
    downwind_mass = slab(mass_pad, 1, face_count, along)
    forward = jnp.maximum(face_flux, 0.0) / upwind_mass
    backward = jnp.maximum(-face_flux, 0.0) / downwind_mass
    from_left = slab(new_right, 0, face_count, along) - 0.5 * forward * (
        slab(edge_jump, 0, face_count, along) - (1.0 - forward * (2.0 / 3.0)) * slab(curvature, 0, face_count, along))
    from_right = slab(new_left, 1, face_count, along) + 0.5 * backward * (
        slab(edge_jump, 1, face_count, along) + (1.0 - backward * (2.0 / 3.0)) * slab(curvature, 1, face_count, along))
    transport = face_flux * jnp.where(face_flux > 0.0, from_left, from_right)
    interior = slab(padded, 3, length, along)
    air_mass = slab(mass_pad, 1, length, along)
    return interior - (slab(transport, 1, length, along) - slab(transport, 0, length, along)) / air_mass


def local_sweep(tracer, face_flux, air_mass, along):
    length = tracer.shape[along]
    return parabola_sweep(pad_axis(tracer, along, 3, 3, "edge"), pad_axis(air_mass, along, 1, 1, "edge"),
                          pad_axis(closed_faces(face_flux, along), along, 1, 0, "constant"), along, length)


def convect(columns, rates, level_axis):
    lower_levels = slab(columns, 0, columns.shape[level_axis] - 1, level_axis)
    moved = rates * lower_levels
    return columns + pad_axis(moved, level_axis, 1, 0, "constant") - pad_axis(moved, level_axis, 0, 1, "constant")


def advect_tracer(single_tracer, x_flux, y_flux, z_flux, air_mass):
    result = parabola_sweep(pad_axis(single_tracer, -2, 3, 3, "wrap"), pad_axis(air_mass, -2, 1, 1, "wrap"),
                            pad_axis(x_flux, -2, 1, 0, "wrap"), -2, single_tracer.shape[-2])
    result = local_sweep(result, y_flux, air_mass, -1)
    return local_sweep(result, z_flux, air_mass, -3)


def reference(tracers, flux_pool, mass_pool, owner, conv_cols, conv_steps, conv_rate):
    flux_tiled = flux_pool.reshape(N_TRC, STEPS, 3, NZ, N_TILE, CX, NY)
    mass_tiled = mass_pool.reshape(N_TRC, STEPS, NZ, N_TILE, CX, NY)
    tile_ids = jnp.arange(N_TILE)
    tile_rows = tile_ids[:, None]
    rates = jnp.transpose(conv_rate, (1, 0, 2))
    state = tracers
    for moment in range(STEPS):
        step_flux = flux_tiled[:, moment]
        step_mass = mass_tiled[:, moment]
        chosen_flux = step_flux[owner[moment], :, :, tile_ids]
        chosen_flux = jnp.transpose(chosen_flux, (1, 2, 0, 3, 4)).reshape(3, NZ, NX, NY)
        chosen_mass = step_mass[owner[moment], :, tile_ids]
        chosen_mass = jnp.transpose(chosen_mass, (1, 0, 2, 3)).reshape(NZ, NX, NY)
        state = lax.map(lambda single_tracer: advect_tracer(single_tracer, chosen_flux[0], chosen_flux[1],
                                                            chosen_flux[2], chosen_mass), state)
        flattened = state.reshape(TRACERS, NZ, N_TILE, CX * NY)
        columns = flattened[:, :, tile_rows, conv_cols]
        for substep in range(3):
            columns = jnp.where(conv_steps > substep, convect(columns, rates, -3), columns)
        state = flattened.at[:, :, tile_rows, conv_cols].set(columns).reshape(TRACERS, NZ, NX, NY)
    return state
```

```python
import jax
import jax.numpy as jnp
from jax import lax
from jax.experimental import pallas as pl
from jax.experimental.pallas import tpu as pltpu
from jax.sharding import Mesh, PartitionSpec as P

TILE = ("x_hi", "y", "core")
TRC = ("x_lo", "za", "zb")
VM = pl.BlockSpec(memory_space=pltpu.VMEM)
F32 = jnp.float32


def shaped(*shape):
    return jax.ShapeDtypeStruct(shape, F32)


def call(kernel, outs, *args, scratch=(), flops=20000, name=None):
    size = sum(4 * a.size for a in args)
    return pl.pallas_call(
        kernel,
        out_shape=outs,
        in_specs=[VM] * len(args),
        out_specs=jax.tree.map(lambda _: VM, outs),
        scratch_shapes=list(scratch),
        cost_estimate=pl.CostEstimate(flops=flops, bytes_accessed=size, transcendentals=0),
        name=name,
    )(*args)


def column(ref, first, x):
    return ref[pl.ds(first + x, 8, stride=8), :]


def pack_kernel(flux_ref, mass_ref, owner_ref, out_ref, owner_out):
    for s in range(2):
        for x in range(8):
            for f in range(3):
                out_ref[f, s, x] = column(flux_ref, (s * 3 + f) * 64, x)
            out_ref[3, s, x] = column(mass_ref, s * 64, x)
        owner_out[s] = jnp.broadcast_to(owner_ref[s : s + 1, 0:1], (8, 128))


def pick_member_kernel(owner_ref, got_ref, out_ref):
    for s in range(2):
        owner = owner_ref[s]
        member = 2 * (owner // 12) + (owner % 2)
        masks = [member == m for m in range(3)]
        for x in range(8):
            value = got_ref[3, s, x]
            for m in range(3):
                value = jnp.where(masks[m], got_ref[m, s, x], value)
            out_ref[s, x] = value


def pick_pair_kernel(owner_ref, got_ref, out_ref):
    for s in range(2):
        pair = (owner_ref[s] % 12) // 2
        masks = [pair == p for p in range(5)]
        for b in range(2):
            for x in range(8):
                value = got_ref[5, b, s, x]
                for p in range(5):
                    value = jnp.where(masks[p], got_ref[p, b, s, x], value)
                out_ref[b, s, x] = value


def convection_kernel(cols_ref, steps_ref, rate_ref, out_ref):
    cols = cols_ref[...]
    at_x, at_y = cols // 128, cols % 128
    values = jnp.concatenate([steps_ref[...].astype(F32), rate_ref[...]], axis=0)
    weights = jnp.concatenate([jnp.where(at_x == x, values, 0.0) for x in range(8)], axis=0)
    hot = jnp.where(lax.broadcasted_iota(jnp.int32, (128, cols.shape[1]), 0) == at_y, 1.0, 0.0)
    dense = lax.dot_general(
        weights, hot, (((1,), (1,)), ((), ())),
        precision=lax.Precision.HIGHEST, preferred_element_type=F32,
    )
    out_ref[...] = dense.reshape(out_ref.shape)


FX, FY, FZ, MASS = range(4)
RIGHT = [(FX, 0, (4, 5, 6, 7)), (MASS, 0, (4, 5, 6, 7)), (FY, 0, (5, 6, 7)), (FZ, 0, (5, 6, 7)), (FX, 1, (7,)), (MASS, 1, (7,))]
LEFT = [(FX, 0, (0, 1, 2)), (MASS, 0, (0, 1, 2, 3)), (FY, 0, (0, 1, 2)), (FZ, 0, (0, 1, 2)), (MASS, 1, (0,))]


def places(plan, offset):
    at, where = 24, {}
    for field, step, columns in plan:
        for x in columns:
            where[field, step, x + offset] = at
            at += 1
    return where, at


FROM_LEFT, CONV_FROM_LEFT = places(RIGHT, -8)
FROM_RIGHT, CONV_FROM_RIGHT = places(LEFT, 8)


def send_kernel(met_ref, tracers_ref, conv_ref, right_ref, left_ref):
    for i in range(4):
        for n in range(6):
            right_ref[6 * i + n] = column(tracers_ref, 64 * i, 2 + n)
            left_ref[6 * i + n] = column(tracers_ref, 64 * i, n)
    for plan, out, conv_columns in ((RIGHT, right_ref, (5, 6, 7)), (LEFT, left_ref, (0, 1, 2))):
        at = 24
        for field, step, columns in plan:
            for x in columns:
                out[at] = met_ref[field, step, x]
                at += 1
        for x in conv_columns:
            out[at] = conv_ref[x]
            at += 1


def clipped(value, bound):
    return jnp.maximum(jnp.minimum(value, jnp.maximum(bound, 0.0)), jnp.minimum(bound, 0.0))


def edge_offset(before, here, after):
    return clipped(0.5 * here + (1.0 / 12.0) * (before - after), here)


def limited(u, v):
    return clipped(u, v + v), clipped(v, u + u)


def face_factors(flux, near, far):
    size = jnp.abs(flux)
    share = size * jnp.where(flux > 0.0, near, far)
    rest = size * (1.0 - share)
    return rest * (1.0 - share), rest * share


def line_sweep(q, flux, k1, k2, per_mass, open_face, axis):
    length = q.shape[axis]

    def ahead(x):
        return pltpu.roll(x, length - 1, axis)

    def behind(x):
        return pltpu.roll(x, 1, axis)

    q_next = ahead(q)
    diff = jnp.where(open_face, q_next - q, 0.0)
    u = edge_offset(behind(diff), diff, ahead(diff))
    v = behind(diff - u)
    u, v = limited(u, v)
    forward = flux > 0.0
    transport = (
        flux * jnp.where(forward, q, q_next)
        + k1 * jnp.where(forward, u, ahead(v))
        + k2 * jnp.where(forward, v, ahead(u))
    )
    return q - (transport - behind(transport)) * per_mass


def sweeps_kernel(met_ref, tracers_ref, conv_ref, left_ref, right_ref, out_ref, state, swept, factors, per_mass, lines):
    lane = lax.broadcasted_iota(jnp.int32, (8, 128), 1)
    level = lax.broadcasted_iota(jnp.int32, (8, 128), 0)
    open_y, open_z = lane < 127, level < 7

    def met(field, step, x):
        if x < 0:
            return left_ref[FROM_LEFT[field, step, x]]
        if x > 7:
            return right_ref[FROM_RIGHT[field, step, x]]
        return met_ref[field, step, x]

    def dense(x):
        if x < 0:
            return left_ref[CONV_FROM_LEFT + 3 + x]
        if x > 7:
            return right_ref[CONV_FROM_RIGHT + x - 8]
        return conv_ref[x]

    def tracer(i, x):
        if x < 0:
            return left_ref[6 * i + 6 + x]
        if x > 7:
            return right_ref[6 * i + x - 8]
        return column(tracers_ref, 64 * i, x)

    for step in range(2):
        lo, hi = (-3, 10) if step == 0 else (0, 7)
        count = hi - lo + 1
        for n in range(count + 2):
            per_mass[n] = 1.0 / met(MASS, step, lo - 1 + n)
        for n in range(count + 1):
            flux = met(FX, step, lo - 1 + n)
            k1, k2 = face_factors(flux, per_mass[n], per_mass[n + 1])
            factors[0, n], factors[1, n], factors[2, n] = flux, k1, k2
        for n in range(count):
            lines[0, n] = met(FY, step, lo + n)
            lines[1, n] = met(FZ, step, lo + n)
            lines[2, n] = dense(lo + n)

        for i in range(4):
            q, diff, u, v, sent = {}, {}, {}, {}, {}
            for e in range(lo - 3, hi + 4):
                q[e] = tracer(i, e) if step == 0 else state[i, e + 3]
                if e - 1 in q:
                    diff[e - 1] = q[e] - q[e - 1]
                if e - 3 in diff:
                    u[e - 2] = edge_offset(diff[e - 3], diff[e - 2], diff[e - 1])
                    v[e - 1] = diff[e - 2] - u[e - 2]
                j = e - 2
                if j in v:
                    u[j], v[j] = limited(u[j], v[j])
                j = e - 3
                if lo - 1 <= j <= hi:
                    n = j - lo + 1
                    flux = factors[0, n]
                    forward = flux > 0.0
                    sent[j] = (
                        flux * jnp.where(forward, q[j], q[j + 1])
                        + factors[1, n] * jnp.where(forward, u[j], v[j + 1])
                        + factors[2, n] * jnp.where(forward, v[j], u[j + 1])
                    )
                if lo <= j <= hi:
                    swept[i, j - lo] = q[j] - (sent[j] - sent[j - 1]) * per_mass[j - lo + 1]

        def across(block, _):
            for m in range(2):
                n = 2 * block + m
                r = per_mass[n + 1]
                fy = jnp.where(open_y, lines[0, n], 0.0)
                y1, y2 = face_factors(fy, r, pltpu.roll(r, 127, 1))
                fz = jnp.where(open_z, lines[1, n], 0.0)
                z1, z2 = face_factors(fz, r, pltpu.roll(r, 7, 0))
                table = lines[2, n]
                substeps = jnp.broadcast_to(table[0:1, :], (8, 128))
                rate = jnp.where(level > 0, table, 0.0)
                rates = [jnp.where(substeps > least, rate, 0.0) for least in (0.5, 1.5, 2.5)]
                keeps = [1.0 - pltpu.roll(part, 7, 0) for part in rates]
                for i in range(4):
                    q = swept[i, n]
                    q = line_sweep(q, fy, y1, y2, r, open_y, 1)
                    q = line_sweep(q, fz, z1, z2, r, open_z, 0)
                    for part, keep in zip(rates, keeps):
                        q = q * keep + part * pltpu.roll(q, 1, 0)
                    if step == 0:
                        state[i, n] = q
                    else:
                        out_ref[pl.ds(64 * i + n, 8, stride=8), :] = q
            return 0

        lax.fori_loop(0, count // 2, across, 0)


def body(tracers, flux_pool, mass_pool, owner, conv_cols, conv_steps, conv_rate):
    packed, owners = call(
        pack_kernel, (shaped(4, 2, 8, 8, 128), jax.ShapeDtypeStruct((2, 8, 128), jnp.int32)),
        flux_pool.reshape(384, 128), mass_pool.reshape(128, 128), owner, name="pack",
    )
    members = lax.all_to_all(packed, ("x_lo", "zb"), 0, 0, tiled=False)
    dense = call(
        convection_kernel, shaped(8, 8, 128), conv_cols, conv_steps, conv_rate[0], flops=30000000, name="convection",
    )
    mine = call(pick_member_kernel, shaped(2, 8, 8, 128), owners, members, name="pick_member")
    pairs = lax.all_gather(mine, ("za", "zb")).reshape(6, 2, 2, 8, 8, 128)
    half = call(pick_pair_kernel, shaped(2, 2, 8, 8, 128), owners, pairs, name="pick_pair")
    met = lax.all_gather(half, "x_lo").reshape(4, 2, 8, 8, 128)
    lines = tracers.reshape(256, 128)
    to_right, to_left = call(
        send_kernel, (shaped(CONV_FROM_LEFT + 3, 8, 128), shaped(CONV_FROM_RIGHT + 3, 8, 128)), met, lines, dense, name="send",
    )
    size = lax.axis_size(TILE)
    up = [(i, (i + 1) % size) for i in range(size)]
    from_left = lax.ppermute(to_right, TILE, up)
    from_right = lax.ppermute(to_left, TILE, [(b, a) for a, b in up])
    out = call(
        sweeps_kernel, shaped(256, 128), met, lines, dense, from_left, from_right,
        scratch=[
            pltpu.VMEM((4, 14, 8, 128), F32), pltpu.VMEM((4, 14, 8, 128), F32), pltpu.VMEM((3, 15, 8, 128), F32),
            pltpu.VMEM((16, 8, 128), F32), pltpu.VMEM((3, 14, 8, 128), F32),
        ],
        name="sweeps",
    )
    return out.reshape(tracers.shape)


def solution(mesh):
    split = Mesh(mesh.devices.reshape(2, 8, 2, 2, 6, 2), TILE + TRC)
    in_specs = (
        P(TRC, None, TILE, None),
        P(TRC, None, None, None, TILE, None),
        P(TRC, None, None, TILE, None),
        P(None, TILE),
        P(TILE, None),
        P(TILE, None),
        P(TILE, None, None),
    )
    out_specs = P(TRC, None, TILE, None)
    return jax.shard_map(body, mesh=split, in_specs=in_specs, out_specs=out_specs, check_vma=False)
```

```python
import jax
import jax.numpy as jnp
from jax import lax
from jax.experimental import pallas as pl
from jax.experimental.pallas import tpu as pltpu
from jax.sharding import Mesh, PartitionSpec as P

TILE = ("x_hi", "y", "core")
TRC = ("x_lo", "za", "zb")
VM = pl.BlockSpec(memory_space=pltpu.VMEM)
F32 = jnp.float32


def shaped(*shape, dtype=F32):
    return pltpu.VMEM(shape, dtype)


def call(kernel, outs, *args, scratch=(), flops=20000, name=None, near=True):
    size = sum(4 * a.size for a in args)
    return pl.pallas_call(
        kernel,
        out_shape=outs,
        in_specs=[VM] * len(args),
        out_specs=jax.tree.map(lambda _: VM, outs),
        scratch_shapes=list(scratch),
        cost_estimate=pl.CostEstimate(flops=flops, bytes_accessed=size, transcendentals=0),
        name=name,
    )(*[pltpu.with_memory_space_constraint(a, pltpu.VMEM) if near else a for a in args])


def column(ref, first, x):
    return ref[pl.ds(first + x, 8, stride=8), :]


def pack_kernel(flux_ref, mass_ref, owner_ref, out_ref, owner_out):
    for s in range(2):
        for x in range(8):
            for f in range(3):
                out_ref[f, s, x] = column(flux_ref, (s * 3 + f) * 64, x)
            out_ref[3, s, x] = column(mass_ref, s * 64, x)
        owner_out[s] = jnp.broadcast_to(owner_ref[0:1, s : s + 1], (8, 128))


def pick_member_kernel(owner_ref, got_ref, out_ref):
    for s in range(2):
        owner = owner_ref[s]
        member = 2 * (owner // 12) + (owner % 2)
        masks = [member == m for m in range(3)]
        for x in range(8):
            value = got_ref[3, s, x]
            for m in range(3):
                value = jnp.where(masks[m], got_ref[m, s, x], value)
            out_ref[s, x] = value


def pick_pair_kernel(owner_ref, got_ref, out_ref):
    for s in range(2):
        pair = (owner_ref[s] % 12) // 2
        masks = [pair == p for p in range(5)]
        for b in range(2):
            for x in range(8):
                value = got_ref[5, b, s, x]
                for p in range(5):
                    value = jnp.where(masks[p], got_ref[p, b, s, x], value)
                out_ref[b, s, x] = value


def convection_kernel(cols_ref, steps_ref, rate_ref, out_ref):
    cols = cols_ref[...]
    at_x, at_y = cols // 128, cols % 128
    values = jnp.concatenate([steps_ref[...].astype(F32), rate_ref[:, 0, :]], axis=0)
    weights = jnp.concatenate([jnp.where(at_x == x, values, 0.0) for x in range(8)], axis=0)
    hot = jnp.where(lax.broadcasted_iota(jnp.int32, (128, cols.shape[1]), 0) == at_y, 1.0, 0.0)
    dense = lax.dot_general(
        weights, hot, (((1,), (1,)), ((), ())),
        precision=lax.Precision.HIGHEST, preferred_element_type=F32,
    )
    out_ref[...] = dense.reshape(out_ref.shape)


FX, FY, FZ, MASS = range(4)
HALO = [(FX, 0, 4), (MASS, 0, 4), (FY, 0, 3), (FZ, 0, 3), (FX, 1, 1), (MASS, 1, 1)]
SENT = 24 + sum(k for _, _, k in HALO) + 3


def send_kernel(met_ref, tracers_ref, conv_ref, far_ref, mate_ref):
    core = lax.axis_index("core")
    for out, last in ((far_ref, core), (mate_ref, 1 - core)):
        for i in range(4):
            for n in range(6):
                out[6 * i + n] = column(tracers_ref, 64 * i, 2 * last + n)
        at = 24
        for field, step, k in HALO:
            for n in range(k):
                out[at + n] = met_ref[field, step, (8 - k) * last + n]
            at += k
        for n in range(3):
            out[at + n] = conv_ref[5 * last + n]


def clipped(value, bound):
    return jnp.maximum(jnp.minimum(value, jnp.maximum(bound, 0.0)), jnp.minimum(bound, 0.0))


def edge_offset(before, here, after):
    return clipped(0.5 * here + (1.0 / 12.0) * (before - after), here)


def limited(u, v):
    return clipped(u, v + v), clipped(v, u + u)


def face_factors(flux, near, far):
    size = jnp.abs(flux)
    share = size * jnp.where(flux > 0.0, near, far)
    rest = size * (1.0 - share)
    return rest * (1.0 - share), rest * share


def line_sweep(q, flux, k1, k2, per_mass, open_face, axis):
    length = q.shape[axis]

    def ahead(x):
        return pltpu.roll(x, length - 1, axis)

    def behind(x):
        return pltpu.roll(x, 1, axis)

    q_next = ahead(q)
    diff = jnp.where(open_face, q_next - q, 0.0)
    u = edge_offset(behind(diff), diff, ahead(diff))
    v = behind(diff - u)
    u, v = limited(u, v)
    forward = flux > 0.0
    transport = (
        flux * jnp.where(forward, q, q_next)
        + k1 * jnp.where(forward, u, ahead(v))
        + k2 * jnp.where(forward, v, ahead(u))
    )
    return q - (transport - behind(transport)) * per_mass


def sweeps_kernel(
    met_ref, tracers_ref, conv_ref, far_ref, mate_ref, out_ref,
    cells, fx_0, mass_0, fy_0, fz_0, fx_1, mass_1, tables, state, swept, factors, per_mass,
):
    lane = lax.broadcasted_iota(jnp.int32, (8, 128), 1)
    level = lax.broadcasted_iota(jnp.int32, (8, 128), 0)
    open_y, open_z = lane < 127, level < 7
    core = lax.axis_index("core")

    wide = {(FX, 0): fx_0, (MASS, 0): mass_0, (FY, 0): fy_0, (FZ, 0): fz_0, (FX, 1): fx_1, (MASS, 1): mass_1}
    for got, right in ((far_ref, core), (mate_ref, 1 - core)):
        for i in range(4):
            for n in range(6):
                cells[i, 14 * right + n] = got[6 * i + n]
        at = 24
        for field, step, k in HALO:
            for n in range(k):
                wide[field, step][(8 + k) * right + n] = got[at + n]
            at += k
        for n in range(3):
            tables[11 * right + n] = got[at + n]
    for x in range(8):
        for i in range(4):
            cells[i, 6 + x] = column(tracers_ref, 64 * i, x)
        for field, step, k in HALO:
            wide[field, step][k + x] = met_ref[field, step, x]
        tables[3 + x] = conv_ref[x]

    for step in range(2):
        lo, hi = (-3, 10) if step == 0 else (0, 7)
        count = hi - lo + 1
        for n in range(count + 2):
            per_mass[n] = 1.0 / wide[MASS, step][n]
        for n in range(count + 1):
            flux = wide[FX, step][n]
            k1, k2 = face_factors(flux, per_mass[n], per_mass[n + 1])
            factors[0, n], factors[1, n], factors[2, n] = flux, k1, k2

        for i in range(4):
            q, diff, u, v, sent = {}, {}, {}, {}, {}
            for e in range(lo - 3, hi + 4):
                q[e] = cells[i, e + 6] if step == 0 else state[i, e + 3]
                if e - 1 in q:
                    diff[e - 1] = q[e] - q[e - 1]
                if e - 3 in diff:
                    u[e - 2] = edge_offset(diff[e - 3], diff[e - 2], diff[e - 1])
                    v[e - 1] = diff[e - 2] - u[e - 2]
                j = e - 2
                if j in v:
                    u[j], v[j] = limited(u[j], v[j])
                j = e - 3
                if lo - 1 <= j <= hi:
                    n = j - lo + 1
                    flux = factors[0, n]
                    forward = flux > 0.0
                    sent[j] = (
                        flux * jnp.where(forward, q[j], q[j + 1])
                        + factors[1, n] * jnp.where(forward, u[j], v[j + 1])
                        + factors[2, n] * jnp.where(forward, v[j], u[j + 1])
                    )
                if lo <= j <= hi:
                    swept[i, j - lo] = q[j] - (sent[j] - sent[j - 1]) * per_mass[j - lo + 1]

        def across(block, _):
            for m in range(2):
                n = 2 * block + m
                r = per_mass[n + 1]
                fy = jnp.where(open_y, fy_0[n] if step == 0 else met_ref[FY, 1, n], 0.0)
                y1, y2 = face_factors(fy, r, pltpu.roll(r, 127, 1))
                fz = jnp.where(open_z, fz_0[n] if step == 0 else met_ref[FZ, 1, n], 0.0)
                z1, z2 = face_factors(fz, r, pltpu.roll(r, 7, 0))
                table = tables[n + 3 + lo]
                substeps = jnp.broadcast_to(table[0:1, :], (8, 128))
                rate = jnp.where(level > 0, table, 0.0)
                rates = [jnp.where(substeps > least, rate, 0.0) for least in (0.5, 1.5, 2.5)]
                keeps = [1.0 - pltpu.roll(part, 7, 0) for part in rates]
                for i in range(4):
                    q = swept[i, n]
                    q = line_sweep(q, fy, y1, y2, r, open_y, 1)
                    q = line_sweep(q, fz, z1, z2, r, open_z, 0)
                    for part, keep in zip(rates, keeps):
                        q = q * keep + part * pltpu.roll(q, 1, 0)
                    if step == 0:
                        state[i, n] = q
                    else:
                        out_ref[pl.ds(64 * i + n, 8, stride=8), :] = q
            return 0

        lax.fori_loop(0, count // 2, across, 0)


def body(tracers, flux_pool, mass_pool, owner, conv_cols, conv_steps, conv_rate):
    packed, owners = call(
        pack_kernel, (shaped(4, 2, 8, 8, 128), shaped(2, 8, 128, dtype=jnp.int32)),
        flux_pool.reshape(384, 128), mass_pool.reshape(128, 128), owner.reshape(1, 2), name="pack", near=False,
    )
    members = lax.all_to_all(packed, ("x_lo", "zb"), 0, 0, tiled=False)
    dense = call(
        convection_kernel, shaped(8, 8, 128), conv_cols, conv_steps, conv_rate.reshape(7, 1, 256), flops=30000000, name="convection",
    )
    mine = call(pick_member_kernel, shaped(2, 8, 8, 128), owners, members, name="pick_member")
    pairs = lax.all_gather(mine, ("za", "zb")).reshape(6, 2, 2, 8, 8, 128)
    half = call(pick_pair_kernel, shaped(2, 2, 8, 8, 128), owners, pairs, name="pick_pair")
    met = lax.all_gather(half, "x_lo").reshape(4, 2, 8, 8, 128)
    lines = tracers.reshape(256, 128)
    to_far, to_mate = call(send_kernel, (shaped(SENT, 8, 128), shaped(SENT, 8, 128)), met, lines, dense, name="send")
    size = lax.axis_size(TILE)
    mates = [(i, i ^ 1) for i in range(size)]
    distant = [(i, (i + 2 * (i % 2) - 1) % size) for i in range(size)]
    from_mate = lax.ppermute(to_mate, TILE, mates)
    from_far = lax.ppermute(to_far, TILE, distant)
    out = call(
        sweeps_kernel, jax.ShapeDtypeStruct((256, 128), F32), met, lines, dense, from_far, from_mate,
        scratch=[pltpu.VMEM((4, 20, 8, 128), F32)]
        + [pltpu.VMEM((8 + 2 * k, 8, 128), F32) for _, _, k in HALO]
        + [pltpu.VMEM((14, 8, 128), F32)]
        + [pltpu.VMEM((n, m, 8, 128), F32) for n, m in ((4, 14), (4, 14), (3, 15))]
        + [pltpu.VMEM((16, 8, 128), F32)],
        name="sweeps",
    )
    return out.reshape(tracers.shape)


def solution(mesh):
    split = Mesh(mesh.devices.reshape(2, 8, 2, 2, 6, 2), TILE + TRC)
    in_specs = (
        P(TRC, None, TILE, None),
        P(TRC, None, None, None, TILE, None),
        P(TRC, None, None, TILE, None),
        P(None, TILE),
        P(TILE, None),
        P(TILE, None),
        P(TILE, None, None),
    )
    out_specs = P(TRC, None, TILE, None)
    return jax.shard_map(body, mesh=split, in_specs=in_specs, out_specs=out_specs, check_vma=False)
```

```python
import jax
import jax.numpy as jnp
from jax import lax
from jax.experimental import pallas as pl
from jax.experimental.pallas import tpu as pltpu
from jax.sharding import Mesh, PartitionSpec as P

TILE = ("x_hi", "y", "core")
TRC = ("x_lo", "z")
VM = pl.BlockSpec(memory_space=pltpu.VMEM)
F32 = jnp.float32


def shaped(*shape, dtype=F32):
    return pltpu.VMEM(shape, dtype)


def call(kernel, outs, *args, scratch=(), flops=20000, name=None, near=True):
    size = sum(4 * a.size for a in args)
    return pl.pallas_call(
        kernel,
        out_shape=outs,
        in_specs=[VM] * len(args),
        out_specs=jax.tree.map(lambda _: VM, outs),
        scratch_shapes=list(scratch),
        cost_estimate=pl.CostEstimate(flops=flops, bytes_accessed=size, transcendentals=0),
        name=name,
    )(*[pltpu.with_memory_space_constraint(a, pltpu.VMEM) if near else a for a in args])


def column(ref, first, x):
    return ref[pl.ds(first + x, 8, stride=8), :]


MEMBERS, SHARE = 24, 3


def pack_kernel(flux_ref, mass_ref, owner_ref, out_ref, owner_out):
    for s in range(2):
        for x in range(8):
            for f in range(3):
                out_ref[32 * s + 8 * f + x] = column(flux_ref, (s * 3 + f) * 64, x)
            out_ref[32 * s + 24 + x] = column(mass_ref, s * 64, x)
        owner_out[s] = jnp.broadcast_to(owner_ref[0:1, s : s + 1], (8, 128))
    for n in range(64, MEMBERS * SHARE):
        out_ref[n] = jnp.zeros((8, 128), F32)


def pick_kernel(owner_ref, got_ref, out_ref):
    me = lax.axis_index(TRC)
    for n in range(SHARE):
        owner = jnp.where(SHARE * me + n < 32, owner_ref[0], owner_ref[1])
        value = got_ref[n]
        for m in range(1, MEMBERS):
            value = jnp.where(owner == m, got_ref[SHARE * m + n], value)
        for m in range(MEMBERS):
            out_ref[SHARE * m + n] = value


def convection_kernel(cols_ref, steps_ref, rate_ref, out_ref):
    cols = cols_ref[...]
    at_x, at_y = cols // 128, cols % 128
    values = jnp.concatenate([steps_ref[...].astype(F32), rate_ref[:, 0, :]], axis=0)
    weights = jnp.concatenate([jnp.where(at_x == x, values, 0.0) for x in range(8)], axis=0)
    hot = jnp.where(lax.broadcasted_iota(jnp.int32, (128, cols.shape[1]), 0) == at_y, 1.0, 0.0)
    dense = lax.dot_general(
        weights, hot, (((1,), (1,)), ((), ())),
        precision=lax.Precision.HIGHEST, preferred_element_type=F32,
    )
    out_ref[...] = dense.reshape(out_ref.shape)


FX, FY, FZ, MASS = range(4)
HALO = [(FX, 0, 4), (MASS, 0, 4), (FY, 0, 3), (FZ, 0, 3), (FX, 1, 1), (MASS, 1, 1)]
SENT = 24 + sum(k for _, _, k in HALO) + 3


def send_kernel(met_ref, tracers_ref, conv_ref, far_ref, mate_ref):
    core = lax.axis_index("core")
    for out, last in ((far_ref, core), (mate_ref, 1 - core)):
        for i in range(4):
            for n in range(6):
                out[6 * i + n] = column(tracers_ref, 64 * i, 2 * last + n)
        at = 24
        for field, step, k in HALO:
            for n in range(k):
                out[at + n] = met_ref[32 * step + 8 * field + (8 - k) * last + n]
            at += k
        for n in range(3):
            out[at + n] = conv_ref[5 * last + n]


def clipped(value, bound):
    return jnp.maximum(jnp.minimum(value, jnp.maximum(bound, 0.0)), jnp.minimum(bound, 0.0))


def edge_offset(before, here, after):
    return clipped(0.5 * here + (1.0 / 12.0) * (before - after), here)


def limited(u, v):
    return clipped(u, v + v), clipped(v, u + u)


def face_factors(flux, near, far):
    size = jnp.abs(flux)
    share = size * jnp.where(flux > 0.0, near, far)
    rest = size * (1.0 - share)
    return rest * (1.0 - share), rest * share


def line_sweep(q, flux, k1, k2, per_mass, open_face, axis):
    length = q.shape[axis]

    def ahead(x):
        return pltpu.roll(x, length - 1, axis)

    def behind(x):
        return pltpu.roll(x, 1, axis)

    q_next = ahead(q)
    diff = jnp.where(open_face, q_next - q, 0.0)
    u = edge_offset(behind(diff), diff, ahead(diff))
    v = behind(diff - u)
    u, v = limited(u, v)
    forward = flux > 0.0
    transport = (
        flux * jnp.where(forward, q, q_next)
        + k1 * jnp.where(forward, u, ahead(v))
        + k2 * jnp.where(forward, v, ahead(u))
    )
    return q - (transport - behind(transport)) * per_mass


def sweeps_kernel(
    met_ref, tracers_ref, conv_ref, far_ref, mate_ref, out_ref,
    cells, fx_0, mass_0, fy_0, fz_0, fx_1, mass_1, tables, state, swept, factors, per_mass,
):
    lane = lax.broadcasted_iota(jnp.int32, (8, 128), 1)
    level = lax.broadcasted_iota(jnp.int32, (8, 128), 0)
    open_y, open_z = lane < 127, level < 7
    core = lax.axis_index("core")

    wide = {(FX, 0): fx_0, (MASS, 0): mass_0, (FY, 0): fy_0, (FZ, 0): fz_0, (FX, 1): fx_1, (MASS, 1): mass_1}
    for got, right in ((far_ref, core), (mate_ref, 1 - core)):
        for i in range(4):
            for n in range(6):
                cells[i, 14 * right + n] = got[6 * i + n]
        at = 24
        for field, step, k in HALO:
            for n in range(k):
                wide[field, step][(8 + k) * right + n] = got[at + n]
            at += k
        for n in range(3):
            tables[11 * right + n] = got[at + n]
    for x in range(8):
        for i in range(4):
            cells[i, 6 + x] = column(tracers_ref, 64 * i, x)
        for field, step, k in HALO:
            wide[field, step][k + x] = met_ref[32 * step + 8 * field + x]
        tables[3 + x] = conv_ref[x]

    for step in range(2):
        lo, hi = (-3, 10) if step == 0 else (0, 7)
        count = hi - lo + 1
        for n in range(count + 2):
            per_mass[n] = 1.0 / wide[MASS, step][n]
        for n in range(count + 1):
            flux = wide[FX, step][n]
            k1, k2 = face_factors(flux, per_mass[n], per_mass[n + 1])
            factors[0, n], factors[1, n], factors[2, n] = flux, k1, k2

        for i in range(4):
            q, diff, u, v, sent = {}, {}, {}, {}, {}
            for e in range(lo - 3, hi + 4):
                q[e] = cells[i, e + 6] if step == 0 else state[i, e + 3]
                if e - 1 in q:
                    diff[e - 1] = q[e] - q[e - 1]
                if e - 3 in diff:
                    u[e - 2] = edge_offset(diff[e - 3], diff[e - 2], diff[e - 1])
                    v[e - 1] = diff[e - 2] - u[e - 2]
                j = e - 2
                if j in v:
                    u[j], v[j] = limited(u[j], v[j])
                j = e - 3
                if lo - 1 <= j <= hi:
                    n = j - lo + 1
                    flux = factors[0, n]
                    forward = flux > 0.0
                    sent[j] = (
                        flux * jnp.where(forward, q[j], q[j + 1])
                        + factors[1, n] * jnp.where(forward, u[j], v[j + 1])
                        + factors[2, n] * jnp.where(forward, v[j], u[j + 1])
                    )
                if lo <= j <= hi:
                    swept[i, j - lo] = q[j] - (sent[j] - sent[j - 1]) * per_mass[j - lo + 1]

        def across(block, _):
            for m in range(2):
                n = 2 * block + m
                r = per_mass[n + 1]
                fy = jnp.where(open_y, fy_0[n] if step == 0 else met_ref[32 + 8 * FY + n], 0.0)
                y1, y2 = face_factors(fy, r, pltpu.roll(r, 127, 1))
                fz = jnp.where(open_z, fz_0[n] if step == 0 else met_ref[32 + 8 * FZ + n], 0.0)
                z1, z2 = face_factors(fz, r, pltpu.roll(r, 7, 0))
                table = tables[n + 3 + lo]
                substeps = jnp.broadcast_to(table[0:1, :], (8, 128))
                rate = jnp.where(level > 0, table, 0.0)
                rates = [jnp.where(substeps > least, rate, 0.0) for least in (0.5, 1.5, 2.5)]
                keeps = [1.0 - pltpu.roll(part, 7, 0) for part in rates]
                for i in range(4):
                    q = swept[i, n]
                    q = line_sweep(q, fy, y1, y2, r, open_y, 1)
                    q = line_sweep(q, fz, z1, z2, r, open_z, 0)
                    for part, keep in zip(rates, keeps):
                        q = q * keep + part * pltpu.roll(q, 1, 0)
                    if step == 0:
                        state[i, n] = q
                    else:
                        out_ref[pl.ds(64 * i + n, 8, stride=8), :] = q
            return 0

        lax.fori_loop(0, count // 2, across, 0)


def body(tracers, flux_pool, mass_pool, owner, conv_cols, conv_steps, conv_rate):
    tiles = MEMBERS * SHARE
    packed, owners = call(
        pack_kernel, (shaped(tiles, 8, 128), shaped(2, 8, 128, dtype=jnp.int32)),
        flux_pool.reshape(384, 128), mass_pool.reshape(128, 128), owner.reshape(1, 2), name="pack", near=False,
    )
    dealt = lax.all_to_all(packed, TRC, 0, 0, tiled=True)
    dense = call(
        convection_kernel, shaped(8, 8, 128), conv_cols, conv_steps, conv_rate.reshape(7, 1, 256), flops=30000000, name="convection",
    )
    picked = call(pick_kernel, shaped(tiles, 8, 128), owners, dealt, name="pick")
    met = lax.all_to_all(picked, TRC, 0, 0, tiled=True)
    lines = tracers.reshape(256, 128)
    to_far, to_mate = call(send_kernel, (shaped(SENT, 8, 128), shaped(SENT, 8, 128)), met, lines, dense, name="send")
    size = lax.axis_size(TILE)
    mates = [(i, i ^ 1) for i in range(size)]
    distant = [(i, (i + 2 * (i % 2) - 1) % size) for i in range(size)]
    from_mate = lax.ppermute(to_mate, TILE, mates)
    from_far = lax.ppermute(to_far, TILE, distant)
    out = call(
        sweeps_kernel, jax.ShapeDtypeStruct((256, 128), F32), met, lines, dense, from_far, from_mate,
        scratch=[pltpu.VMEM((4, 20, 8, 128), F32)]
        + [pltpu.VMEM((8 + 2 * k, 8, 128), F32) for _, _, k in HALO]
        + [pltpu.VMEM((14, 8, 128), F32)]
        + [pltpu.VMEM((n, m, 8, 128), F32) for n, m in ((4, 14), (4, 14), (3, 15))]
        + [pltpu.VMEM((16, 8, 128), F32)],
        name="sweeps",
    )
    return out.reshape(tracers.shape)


def solution(mesh):
    split = Mesh(mesh.devices.reshape(2, 8, 2, 2, 12), TILE + TRC)
    in_specs = (
        P(TRC, None, TILE, None),
        P(TRC, None, None, None, TILE, None),
        P(TRC, None, None, TILE, None),
        P(None, TILE),
        P(TILE, None),
        P(TILE, None),
        P(TILE, None, None),
    )
    out_specs = P(TRC, None, TILE, None)
    return jax.shard_map(body, mesh=split, in_specs=in_specs, out_specs=out_specs, check_vma=False)
```

```python
import functools

import jax
import jax.numpy as jnp
from jax import lax
from jax.experimental import pallas as pl
from jax.experimental.pallas import tpu as pltpu
from jax.sharding import Mesh, PartitionSpec as P

TILE = ("x_hi", "y", "core")
TRC = ("x_lo", "za", "zb")
NEAR = ("x_lo", "zb")
VM = pl.BlockSpec(memory_space=pltpu.VMEM)
F32 = jnp.float32


def shaped(*shape, dtype=F32):
    return pltpu.VMEM(shape, dtype)


def call(kernel, outs, *args, scratch=(), flops=20000, near=True):
    size = sum(4 * a.size for a in args)
    return pl.pallas_call(
        kernel,
        out_shape=outs,
        in_specs=[VM] * len(args),
        out_specs=jax.tree.map(lambda _: VM, outs),
        scratch_shapes=list(scratch),
        cost_estimate=pl.CostEstimate(flops=flops, bytes_accessed=size, transcendentals=0),
    )(*[pltpu.with_memory_space_constraint(a, pltpu.VMEM) if near else a for a in args])


def column(ref, first, x):
    return ref[pl.ds(first + x, 8, stride=8), :]


def pack_kernel(flux_ref, mass_ref, owner_ref, cols_ref, steps_ref, rate_ref, out_ref, owner_out, dense_ref):
    for s in range(2):
        for x in range(8):
            for f in range(3):
                out_ref[32 * s + 8 * f + x] = column(flux_ref, (s * 3 + f) * 64, x)
            out_ref[32 * s + 24 + x] = column(mass_ref, s * 64, x)
    first = lax.axis_index("x_lo") == 0
    owner = jnp.broadcast_to(jnp.where(first, owner_ref[0:1, 0:1], owner_ref[0:1, 1:2]), (8, 128))
    owner_out[0] = 4 * (owner // 12) + owner % 4
    owner_out[1] = (owner % 12) // 4
    cols = cols_ref[...]
    at_x, at_y = cols // 128, cols % 128
    values = jnp.concatenate([steps_ref[...].astype(F32), rate_ref[:, 0, :]], axis=0)
    weights = jnp.concatenate([jnp.where(at_x == x, values, 0.0) for x in range(8)], axis=0)
    hot = jnp.where(lax.broadcasted_iota(jnp.int32, (128, cols.shape[1]), 0) == at_y, 1.0, 0.0)
    dense = lax.dot_general(
        weights, hot, (((1,), (1,)), ((), ())),
        precision=lax.Precision.HIGHEST, preferred_element_type=F32,
    )
    dense_ref[...] = dense.reshape(dense_ref.shape)


def pick_kernel(owner_ref, got_ref, out_ref, *, which):
    owner = owner_ref[which]
    copies = out_ref.shape[0] // 8
    for n in range(8):
        value = got_ref[n]
        for m in range(1, got_ref.shape[0] // 8):
            value = jnp.where(owner == m, got_ref[8 * m + n], value)
        for m in range(copies):
            out_ref[8 * m + n] = value


FX, FY, FZ, MASS = range(4)
HALO = [(FX, 0, 4), (MASS, 0, 4), (FY, 0, 3), (FZ, 0, 3), (FX, 1, 1), (MASS, 1, 1)]
SENT = 24 + sum(k for _, _, k in HALO) + 3


def send_kernel(met_ref, tracers_ref, conv_ref, far_ref, mate_ref):
    core = lax.axis_index("core")
    for out, last in ((far_ref, core), (mate_ref, 1 - core)):
        for i in range(4):
            for n in range(6):
                out[6 * i + n] = column(tracers_ref, 64 * i, 2 * last + n)
        at = 24
        for field, step, k in HALO:
            for n in range(k):
                out[at + n] = met_ref[32 * step + 8 * field + (8 - k) * last + n]
            at += k
        for n in range(3):
            out[at + n] = conv_ref[5 * last + n]


def clipped(value, bound):
    return jnp.maximum(jnp.minimum(value, jnp.maximum(bound, 0.0)), jnp.minimum(bound, 0.0))


def edge_offset(before, here, after):
    return clipped(0.5 * here + (1.0 / 12.0) * (before - after), here)


def limited(u, v):
    return clipped(u, v + v), clipped(v, u + u)


def face_factors(flux, near, far):
    size = jnp.abs(flux)
    share = size * jnp.where(flux > 0.0, near, far)
    rest = size * (1.0 - share)
    return rest * (1.0 - share), rest * share


def line_sweep(q, flux, k1, k2, per_mass, open_face, axis):
    length = q.shape[axis]

    def ahead(x):
        return pltpu.roll(x, length - 1, axis)

    def behind(x):
        return pltpu.roll(x, 1, axis)

    q_next = ahead(q)
    diff = jnp.where(open_face, q_next - q, 0.0)
    u = edge_offset(behind(diff), diff, ahead(diff))
    v = behind(diff - u)
    u, v = limited(u, v)
    forward = flux > 0.0
    transport = (
        flux * jnp.where(forward, q, q_next)
        + k1 * jnp.where(forward, u, ahead(v))
        + k2 * jnp.where(forward, v, ahead(u))
    )
    return q - (transport - behind(transport)) * per_mass


def stage(wide, cells, tables, met_ref, tracers_ref, conv_ref, halos):
    for got, right in halos:
        if cells is not None:
            for i in range(4):
                for n in range(6):
                    cells[i, 14 * right + n] = got[6 * i + n]
            for n in range(3):
                tables[11 * right + n] = got[SENT - 3 + n]
        at = 24
        for field, step, k in HALO:
            if (field, step) in wide:
                for n in range(k):
                    wide[field, step][(8 + k) * right + n] = got[at + n]
            at += k
    for x in range(8):
        if cells is not None:
            for i in range(4):
                cells[i, 6 + x] = column(tracers_ref, 64 * i, x)
            tables[3 + x] = conv_ref[x]
        for field, step, k in HALO:
            if (field, step) in wide:
                wide[field, step][k + x] = met_ref[32 * step + 8 * field + x]


def advance(count, cell, flux_x, mass, flux_y, flux_z, table, emit, swept, factors, per_mass, group=2):
    lane = lax.broadcasted_iota(jnp.int32, (8, 128), 1)
    level = lax.broadcasted_iota(jnp.int32, (8, 128), 0)
    open_y, open_z = lane < 127, level < 7
    for n in range(count + 2):
        per_mass[n] = 1.0 / mass(n)
    for n in range(count + 1):
        flux = flux_x(n)
        k1, k2 = face_factors(flux, per_mass[n], per_mass[n + 1])
        factors[0, n], factors[1, n], factors[2, n] = flux, k1, k2

    for i in range(4):
        q, diff, u, v, sent = {}, {}, {}, {}, {}
        for e in range(-3, count + 3):
            q[e] = cell(i, e + 3)
            if e - 1 in q:
                diff[e - 1] = q[e] - q[e - 1]
            if e - 3 in diff:
                u[e - 2] = edge_offset(diff[e - 3], diff[e - 2], diff[e - 1])
                v[e - 1] = diff[e - 2] - u[e - 2]
            j = e - 2
            if j in v:
                u[j], v[j] = limited(u[j], v[j])
            j = e - 3
            if -1 <= j < count:
                flux = factors[0, j + 1]
                forward = flux > 0.0
                sent[j] = (
                    flux * jnp.where(forward, q[j], q[j + 1])
                    + factors[1, j + 1] * jnp.where(forward, u[j], v[j + 1])
                    + factors[2, j + 1] * jnp.where(forward, v[j], u[j + 1])
                )
            if 0 <= j < count:
                swept[i, j] = q[j] - (sent[j] - sent[j - 1]) * per_mass[j + 1]

    def across(block, _):
        for m in range(group):
            n = group * block + m
            r = per_mass[n + 1]
            fy = jnp.where(open_y, flux_y(n), 0.0)
            y1, y2 = face_factors(fy, r, pltpu.roll(r, 127, 1))
            fz = jnp.where(open_z, flux_z(n), 0.0)
            z1, z2 = face_factors(fz, r, pltpu.roll(r, 7, 0))
            dense = table(n)
            substeps = jnp.broadcast_to(dense[0:1, :], (8, 128))
            rate = jnp.where(level > 0, dense, 0.0)
            rates = [jnp.where(substeps > least, rate, 0.0) for least in (0.5, 1.5, 2.5)]
            keeps = [1.0 - pltpu.roll(part, 7, 0) for part in rates]
            for i in range(4):
                q = swept[i, n]
                q = line_sweep(q, fy, y1, y2, r, open_y, 1)
                q = line_sweep(q, fz, z1, z2, r, open_z, 0)
                for part, keep in zip(rates, keeps):
                    q = q * keep + part * pltpu.roll(q, 1, 0)
                emit(i, n, q)
        return 0

    lax.fori_loop(0, count // group, across, 0)


def near_kernel(
    met_ref, tracers_ref, conv_ref, mate_ref, out_ref,
    cells, fx_0, mass_0, fy_0, fz_0, tables, swept, factors, per_mass,
):
    core = lax.axis_index("core")
    wide = {(FX, 0): fx_0, (MASS, 0): mass_0, (FY, 0): fy_0, (FZ, 0): fz_0}
    stage(wide, cells, tables, met_ref, tracers_ref, conv_ref, ((mate_ref, 1 - core),))
    base = 6 * (1 - core)

    def emit(i, n, q):
        out_ref[i, n] = q

    advance(
        8, lambda i, n: cells[i, base + n], lambda n: fx_0[base + n], lambda n: mass_0[base + n],
        lambda n: fy_0[base + n], lambda n: fz_0[base + n], lambda n: tables[base + n], emit, swept, factors, per_mass,
    )


def far_kernel(
    met_ref, tracers_ref, conv_ref, mate_ref, far_ref, near_ref, out_ref,
    cells, fx_0, mass_0, fy_0, fz_0, fx_1, mass_1, tables, state, swept, factors, per_mass,
):
    core = lax.axis_index("core")
    wide = {(FX, 0): fx_0, (MASS, 0): mass_0, (FY, 0): fy_0, (FZ, 0): fz_0}
    stage(wide, cells, tables, met_ref, tracers_ref, conv_ref, ((far_ref, core),))
    stage({(FX, 1): fx_1, (MASS, 1): mass_1}, None, None, met_ref, None, None, ((far_ref, core), (mate_ref, 1 - core)))
    base = 8 * core

    def keep(i, n, q):
        state[i, base + n] = q

    for i in range(4):
        for n in range(8):
            state[i, 6 * (1 - core) + n] = near_ref[i, n]
    advance(
        6, lambda i, n: cells[i, base + n], lambda n: fx_0[base + n], lambda n: mass_0[base + n],
        lambda n: fy_0[base + n], lambda n: fz_0[base + n], lambda n: tables[base + n], keep, swept, factors, per_mass,
    )

    def emit(i, n, q):
        out_ref[pl.ds(64 * i + n, 8, stride=8), :] = q

    advance(
        8, lambda i, n: state[i, n], lambda n: fx_1[n], lambda n: mass_1[n],
        lambda n: met_ref[32 + 8 * FY + n], lambda n: met_ref[32 + 8 * FZ + n], lambda n: tables[3 + n], emit, swept, factors, per_mass,
    )


def body(tracers, flux_pool, mass_pool, owner, conv_cols, conv_steps, conv_rate):
    packed, owners, dense = call(
        pack_kernel, (shaped(64, 8, 128), shaped(2, 8, 128, dtype=jnp.int32), shaped(8, 8, 128)),
        flux_pool.reshape(384, 128), mass_pool.reshape(128, 128), owner.reshape(1, 2),
        conv_cols, conv_steps, conv_rate.reshape(7, 1, 256), near=False,
    )
    dealt = lax.all_to_all(packed, NEAR, 0, 0, tiled=True)
    third = call(functools.partial(pick_kernel, which=0), shaped(24, 8, 128), owners, dealt)
    thirds = lax.all_to_all(third, "za", 0, 0, tiled=True)
    own = call(functools.partial(pick_kernel, which=1), shaped(64, 8, 128), owners, thirds)
    met = lax.all_to_all(own, NEAR, 0, 0, tiled=True)
    lines = tracers.reshape(256, 128)
    to_far, to_mate = call(send_kernel, (shaped(SENT, 8, 128), shaped(SENT, 8, 128)), met, lines, dense)
    size = lax.axis_size(TILE)
    mates = [(i, i ^ 1) for i in range(size)]
    distant = [(i, (i + 2 * (i % 2) - 1) % size) for i in range(size)]
    from_mate = lax.ppermute(to_mate, TILE, mates)
    from_far = lax.ppermute(to_far, TILE, distant)
    arrays = [pltpu.VMEM((4, 20, 8, 128), F32)] + [pltpu.VMEM((8 + 2 * k, 8, 128), F32) for _, _, k in HALO[:4]]
    work = [pltpu.VMEM((4, 8, 8, 128), F32), pltpu.VMEM((3, 9, 8, 128), F32), pltpu.VMEM((10, 8, 128), F32)]
    ahead = call(
        near_kernel, shaped(4, 8, 8, 128), met, lines, dense, from_mate,
        scratch=arrays + [pltpu.VMEM((14, 8, 128), F32)] + work, flops=3000000,
    )
    out = call(
        far_kernel, jax.ShapeDtypeStruct((256, 128), F32), met, lines, dense, from_mate, from_far, ahead,
        scratch=arrays + [pltpu.VMEM((10, 8, 128), F32)] * 2 + [pltpu.VMEM((14, 8, 128), F32), pltpu.VMEM((4, 14, 8, 128), F32)] + work,
        flops=5000000,
    )
    return out.reshape(tracers.shape)


def solution(mesh):
    split = Mesh(mesh.devices.reshape(2, 8, 2, 2, 3, 4), TILE + TRC)
    in_specs = (
        P(TRC, None, TILE, None),
        P(TRC, None, None, None, TILE, None),
        P(TRC, None, None, TILE, None),
        P(None, TILE),
        P(TILE, None),
        P(TILE, None),
        P(TILE, None, None),
    )
    out_specs = P(TRC, None, TILE, None)
    return jax.shard_map(body, mesh=split, in_specs=in_specs, out_specs=out_specs, check_vma=False)
```

```python
import functools

import jax
import jax.numpy as jnp
from jax import lax
from jax.experimental import pallas as pl
from jax.experimental.pallas import tpu as pltpu
from jax.sharding import Mesh, PartitionSpec as P

TILE = ("x_hi", "y", "core")
TRC = ("x_lo", "za", "zb")
NEAR = ("x_lo", "zb")
VM = pl.BlockSpec(memory_space=pltpu.VMEM)
F32 = jnp.float32


def shaped(*shape, dtype=F32):
    return pltpu.VMEM(shape, dtype)


def call(kernel, outs, *args, scratch=(), flops=20000, near=True):
    size = sum(4 * a.size for a in args)
    return pl.pallas_call(
        kernel,
        out_shape=outs,
        in_specs=[VM] * len(args),
        out_specs=jax.tree.map(lambda _: VM, outs),
        scratch_shapes=list(scratch),
        cost_estimate=pl.CostEstimate(flops=flops, bytes_accessed=size, transcendentals=0),
    )(*[pltpu.with_memory_space_constraint(a, pltpu.VMEM) if near else a for a in args])


def column(ref, first, x):
    return ref[pl.ds(first + x, 8, stride=8), :]


def pack_kernel(flux_ref, mass_ref, owner_ref, cols_ref, steps_ref, rate_ref, out_ref, owner_out, dense_ref):
    for s in range(2):
        for x in range(8):
            for f in range(3):
                out_ref[32 * s + 8 * f + x] = column(flux_ref, (s * 3 + f) * 64, x)
            out_ref[32 * s + 24 + x] = column(mass_ref, s * 64, x)
    first = lax.axis_index("x_lo") == 0
    owner = jnp.broadcast_to(jnp.where(first, owner_ref[0:1, 0:1], owner_ref[0:1, 1:2]), (8, 128))
    owner_out[0] = 4 * (owner // 12) + owner % 4
    owner_out[1] = (owner % 12) // 4
    cols = cols_ref[...]
    at_x, at_y = cols // 128, cols % 128
    values = jnp.concatenate([steps_ref[...].astype(F32), rate_ref[:, 0, :]], axis=0)
    weights = jnp.concatenate([jnp.where(at_x == x, values, 0.0) for x in range(8)], axis=0)
    hot = jnp.where(lax.broadcasted_iota(jnp.int32, (128, cols.shape[1]), 0) == at_y, 1.0, 0.0)
    dense = lax.dot_general(
        weights, hot, (((1,), (1,)), ((), ())),
        precision=lax.Precision.HIGHEST, preferred_element_type=F32,
    )
    dense_ref[...] = dense.reshape(dense_ref.shape)


def pick_kernel(owner_ref, got_ref, out_ref, *, which):
    owner = owner_ref[which]
    copies = out_ref.shape[0] // 8
    for n in range(8):
        value = got_ref[n]
        for m in range(1, got_ref.shape[0] // 8):
            value = jnp.where(owner == m, got_ref[8 * m + n], value)
        for m in range(copies):
            out_ref[8 * m + n] = value


def rows(n):
    return pl.ds(8 * n if isinstance(n, int) else pl.multiple_of(8 * n, 8), 8), slice(None)


FX, FY, FZ, MASS = range(4)
HALO = [(FX, 0, 4), (MASS, 0, 4), (FY, 0, 3), (FZ, 0, 3), (FX, 1, 1), (MASS, 1, 1)]
SENT = 24 + sum(k for _, _, k in HALO) + 3


def send_kernel(met_ref, tracers_ref, conv_ref, far_ref, mate_ref):
    core = lax.axis_index("core")
    for out, last in ((far_ref, core), (mate_ref, 1 - core)):
        for i in range(4):
            for n in range(6):
                out[6 * i + n] = column(tracers_ref, 64 * i, 2 * last + n)
        at = 24
        for field, step, k in HALO:
            for n in range(k):
                out[at + n] = met_ref[32 * step + 8 * field + (8 - k) * last + n]
            at += k
        for n in range(3):
            out[at + n] = conv_ref[5 * last + n]


def clipped(value, bound):
    return jnp.maximum(jnp.minimum(value, jnp.maximum(bound, 0.0)), jnp.minimum(bound, 0.0))


def edge_offset(before, here, after):
    return clipped(0.5 * here + (1.0 / 12.0) * (before - after), here)


def limited(u, v):
    return clipped(u, v + v), clipped(v, u + u)


def face_factors(flux, near, far):
    size = jnp.abs(flux)
    share = size * jnp.where(flux > 0.0, near, far)
    rest = size * (1.0 - share)
    return rest * (1.0 - share), rest * share


def sweep_y(q, flux, k1, k2, per_mass, open_face):
    def ahead(x):
        return pltpu.roll(x, 127, 1)

    def behind(x):
        return pltpu.roll(x, 1, 1)

    q_next = ahead(q)
    diff = jnp.where(open_face, q_next - q, 0.0)
    u = edge_offset(behind(diff), diff, ahead(diff))
    v = behind(diff - u)
    u, v = limited(u, v)
    forward = flux > 0.0
    transport = (
        flux * jnp.where(forward, q, q_next)
        + k1 * jnp.where(forward, u, ahead(v))
        + k2 * jnp.where(forward, v, ahead(u))
    )
    return q - (transport - behind(transport)) * per_mass


def sweep_z(q, faces, per_mass):
    diff = [q[k + 1] - q[k] for k in range(7)]
    zero = jnp.zeros_like(q[0])
    u, v = [zero] * 8, [zero] * 8
    edge, rest = {}, {}
    for k in range(7):
        slope = diff[k - 1] - diff[k + 1] if 0 < k < 6 else (-diff[1] if k == 0 else diff[5])
        edge[k] = clipped(0.5 * diff[k] + (1.0 / 12.0) * slope, diff[k])
        rest[k + 1] = diff[k] - edge[k]
        if k > 0:
            u[k], v[k] = limited(edge[k], rest[k])
    out, before = [], None
    for k in range(8):
        if k < 7:
            flux, k1, k2 = faces(k)
            forward = flux > 0.0
            sent = (
                flux * jnp.where(forward, q[k], q[k + 1])
                + k1 * jnp.where(forward, u[k], v[k + 1])
                + k2 * jnp.where(forward, v[k], u[k + 1])
            )
            change = sent if before is None else sent - before
            before = sent
        else:
            change = -before
        out.append(q[k] - change * per_mass(k))
    return out


def stage(wide, cells, tables, met_ref, tracers_ref, conv_ref, halos):
    for got, right in halos:
        if cells is not None:
            for i in range(4):
                for n in range(6):
                    cells[rows(20 * i + 14 * right + n)] = got[6 * i + n]
            for n in range(3):
                tables[rows(11 * right + n)] = got[SENT - 3 + n]
        at = 24
        for field, step, k in HALO:
            if (field, step) in wide:
                for n in range(k):
                    wide[field, step][rows((8 + k) * right + n)] = got[at + n]
            at += k
    for x in range(8):
        if cells is not None:
            for i in range(4):
                cells[rows(20 * i + 6 + x)] = column(tracers_ref, 64 * i, x)
            tables[rows(3 + x)] = conv_ref[x]
        for field, step, k in HALO:
            if (field, step) in wide:
                wide[field, step][rows(k + x)] = met_ref[rows(32 * step + 8 * field + x)]


def level(ref, first, k):
    return ref[pl.ds(8 * first + k, 8, stride=8), :]


def advance(count, shift, cell, flux_x, mass, flux_y, flux_z, tables, window, emit, swept, factors, per_mass, lines):
    for n in range(count + 2):
        per_mass[rows(n + 2)] = 1.0 / mass(n)
    for n in range(count + 1):
        flux = flux_x(n)
        k1, k2 = face_factors(flux, per_mass[rows(n + 2)], per_mass[rows(n + 3)])
        factors[0, n], factors[1, n], factors[2, n] = flux, k1, k2

    for i in range(4):
        q, diff, u, v, sent = {}, {}, {}, {}, {}
        for e in range(-3, count + 3):
            q[e] = cell(i, e + 3)
            if e - 1 in q:
                diff[e - 1] = q[e] - q[e - 1]
            if e - 3 in diff:
                u[e - 2] = edge_offset(diff[e - 3], diff[e - 2], diff[e - 1])
                v[e - 1] = diff[e - 2] - u[e - 2]
            j = e - 2
            if j in v:
                u[j], v[j] = limited(u[j], v[j])
            j = e - 3
            if -1 <= j < count:
                flux = factors[0, j + 1]
                forward = flux > 0.0
                sent[j] = (
                    flux * jnp.where(forward, q[j], q[j + 1])
                    + factors[1, j + 1] * jnp.where(forward, u[j], v[j + 1])
                    + factors[2, j + 1] * jnp.where(forward, v[j], u[j + 1])
                )
            if 0 <= j < count:
                swept[rows(8 * i + j + shift)] = q[j] - (sent[j] - sent[j - 1]) * per_mass[rows(j + 3)]

    open_y = lax.broadcasted_iota(jnp.int32, (8, 128), 1) < 127
    substeps = level(tables, window, 0)
    for k in range(8):
        r = level(per_mass, 3 - shift, k)
        fy = jnp.where(open_y, flux_y(k), 0.0)
        y1, y2 = face_factors(fy, r, pltpu.roll(r, 127, 1))
        lines[0, k], lines[1, k], lines[2, k], lines[3, k] = r, fy, y1, y2
        if k > 0:
            fz = flux_z(k - 1)
            z1, z2 = face_factors(fz, r_below, r)
            lines[4, k - 1], lines[5, k - 1], lines[6, k - 1] = fz, z1, z2
            rate = level(tables, window, k)
            lines[7, k] = rate
            lines[8, k] = jnp.where(substeps > 1.5, rate, 0.0)
            lines[9, k] = jnp.where(substeps > 2.5, rate, 0.0)
        r_below = r

    for i in range(4):
        q = [level(swept, 8 * i, k) for k in range(8)]
        q = [sweep_y(q[k], lines[1, k], lines[2, k], lines[3, k], lines[0, k], open_y) for k in range(8)]
        q = sweep_z(q, lambda k: (lines[4, k], lines[5, k], lines[6, k]), lambda k: lines[0, k])
        for m in (7, 8, 9):
            up = [None] + [lines[m, k] for k in range(1, 8)]
            q = [
                (q[k] * (1.0 - up[k + 1]) if k < 7 else q[k]) + (up[k] * q[k - 1] if k > 0 else 0.0)
                for k in range(8)
            ]
        for k in range(8):
            emit(i, k, q[k])


def near_kernel(
    met_ref, tracers_ref, conv_ref, mate_ref, out_ref,
    cells, fx_0, mass_0, fy_0, fz_0, tables, swept, factors, per_mass, lines,
):
    core = lax.axis_index("core")
    wide = {(FX, 0): fx_0, (MASS, 0): mass_0, (FY, 0): fy_0, (FZ, 0): fz_0}
    stage(wide, cells, tables, met_ref, tracers_ref, conv_ref, ((mate_ref, 1 - core),))
    base = 6 * (1 - core)

    def emit(i, k, q):
        out_ref[pl.ds(64 * i + k, 8, stride=8), :] = q

    advance(
        8, 0, lambda i, n: cells[rows(20 * i + base + n)], lambda n: fx_0[rows(base + n)], lambda n: mass_0[rows(base + n)],
        lambda k: level(fy_0, base, k), lambda k: level(fz_0, base, k), tables, base, emit, swept, factors, per_mass, lines,
    )


def far_kernel(
    met_ref, tracers_ref, conv_ref, mate_ref, far_ref, near_ref, out_ref,
    cells, fx_0, mass_0, fy_0, fz_0, fx_1, mass_1, tables, state, swept, factors, per_mass, lines,
):
    core = lax.axis_index("core")
    wide = {(FX, 0): fx_0, (MASS, 0): mass_0, (FY, 0): fy_0, (FZ, 0): fz_0}
    stage(wide, cells, tables, met_ref, tracers_ref, conv_ref, ((far_ref, core),))
    stage({(FX, 1): fx_1, (MASS, 1): mass_1}, None, None, met_ref, None, None, ((far_ref, core), (mate_ref, 1 - core)))
    base, window = 8 * core, 6 * core

    def keep(i, k, q):
        state[pl.ds(8 * (14 * i + window) + k, 8, stride=8), :] = q

    advance(
        6, 2 * core, lambda i, n: cells[rows(20 * i + base + n)], lambda n: fx_0[rows(base + n)], lambda n: mass_0[rows(base + n)],
        lambda k: level(fy_0, window, k), lambda k: level(fz_0, window, k), tables, window, keep, swept, factors, per_mass, lines,
    )
    for i in range(4):
        for n in range(8):
            state[rows(14 * i + 6 * (1 - core) + n)] = near_ref[rows(8 * i + n)]

    def emit(i, k, q):
        out_ref[rows(8 * i + k)] = q

    advance(
        8, 0, lambda i, n: state[rows(14 * i + n)], lambda n: fx_1[rows(n)], lambda n: mass_1[rows(n)],
        lambda k: level(met_ref, 32 + 8 * FY, k), lambda k: level(met_ref, 32 + 8 * FZ, k), tables, 3, emit, swept, factors, per_mass, lines,
    )


def body(tracers, flux_pool, mass_pool, owner, conv_cols, conv_steps, conv_rate):
    packed, owners, dense = call(
        pack_kernel, (shaped(64, 8, 128), shaped(2, 8, 128, dtype=jnp.int32), shaped(8, 8, 128)),
        flux_pool.reshape(384, 128), mass_pool.reshape(128, 128), owner.reshape(1, 2),
        conv_cols, conv_steps, conv_rate.reshape(7, 1, 256), near=False,
    )
    dealt = lax.all_to_all(packed, NEAR, 0, 0, tiled=True)
    third = call(functools.partial(pick_kernel, which=0), shaped(24, 8, 128), owners, dealt)
    thirds = lax.all_to_all(third, "za", 0, 0, tiled=True)
    own = call(functools.partial(pick_kernel, which=1), shaped(64, 8, 128), owners, thirds)
    met = lax.all_to_all(own, NEAR, 0, 0, tiled=True)
    lines = tracers.reshape(256, 128)
    to_far, to_mate = call(send_kernel, (shaped(SENT, 8, 128), shaped(SENT, 8, 128)), met, lines, dense)
    size = lax.axis_size(TILE)
    mates = [(i, i ^ 1) for i in range(size)]
    distant = [(i, (i + 2 * (i % 2) - 1) % size) for i in range(size)]
    from_mate = lax.ppermute(to_mate, TILE, mates)
    from_far = lax.ppermute(to_far, TILE, distant)

    def columns(n):
        return pltpu.VMEM((8 * n, 128), F32)

    met = met.reshape(512, 128)
    arrays = [columns(80)] + [columns(8 + 2 * k) for _, _, k in HALO[:4]]
    work = [columns(32), pltpu.VMEM((3, 9, 8, 128), F32), columns(12), pltpu.VMEM((10, 8, 8, 128), F32)]
    ahead = call(
        near_kernel, shaped(256, 128), met, lines, dense, from_mate,
        scratch=arrays + [columns(14)] + work, flops=3000000,
    )
    out = call(
        far_kernel, jax.ShapeDtypeStruct((256, 128), F32), met, lines, dense, from_mate, from_far, ahead,
        scratch=arrays + [columns(10)] * 2 + [columns(14), columns(56)] + work, flops=5000000,
    )
    return out.reshape(tracers.shape)


def solution(mesh):
    split = Mesh(mesh.devices.reshape(2, 8, 2, 2, 3, 4), TILE + TRC)
    in_specs = (
        P(TRC, None, TILE, None),
        P(TRC, None, None, None, TILE, None),
        P(TRC, None, None, TILE, None),
        P(None, TILE),
        P(TILE, None),
        P(TILE, None),
        P(TILE, None, None),
    )
    out_specs = P(TRC, None, TILE, None)
    return jax.shard_map(body, mesh=split, in_specs=in_specs, out_specs=out_specs, check_vma=False)
```

```python
import functools

import jax
import jax.numpy as jnp
from jax import lax
from jax.experimental import pallas as pl
from jax.experimental.pallas import tpu as pltpu
from jax.sharding import Mesh, PartitionSpec as P

TILE = ("x_hi", "y", "core")
TRC = ("x_lo", "za", "zb")
NEAR = ("x_lo", "zb")
VM = pl.BlockSpec(memory_space=pltpu.VMEM)
F32 = jnp.float32


def shaped(*shape, dtype=F32):
    return pltpu.VMEM(shape, dtype)


def call(kernel, outs, *args, scratch=(), flops=20000, near=True):
    size = sum(4 * a.size for a in args)
    return pl.pallas_call(
        kernel,
        out_shape=outs,
        in_specs=[VM] * len(args),
        out_specs=jax.tree.map(lambda _: VM, outs),
        scratch_shapes=list(scratch),
        cost_estimate=pl.CostEstimate(flops=flops, bytes_accessed=size, transcendentals=0),
    )(*[pltpu.with_memory_space_constraint(a, pltpu.VMEM) if near else a for a in args])


def column(ref, first, x):
    return ref[pl.ds(first + x, 8, stride=8), :]


def pack_kernel(flux_ref, mass_ref, owner_ref, cols_ref, steps_ref, rate_ref, out_ref, owner_out, dense_ref):
    for s in range(2):
        for x in range(8):
            for f in range(3):
                out_ref[32 * s + 8 * f + x] = column(flux_ref, (s * 3 + f) * 64, x)
            out_ref[32 * s + 24 + x] = column(mass_ref, s * 64, x)
    first = lax.axis_index("x_lo") == 0
    owner = jnp.broadcast_to(jnp.where(first, owner_ref[0:1, 0:1], owner_ref[0:1, 1:2]), (8, 128))
    owner_out[0] = 4 * (owner // 12) + owner % 4
    owner_out[1] = (owner % 12) // 4
    cols = cols_ref[...]
    at_x, at_y = cols // 128, cols % 128
    values = jnp.concatenate([steps_ref[...].astype(F32), rate_ref[:, 0, :]], axis=0)
    weights = jnp.concatenate([jnp.where(at_x == x, values, 0.0) for x in range(8)], axis=0)
    hot = jnp.where(lax.broadcasted_iota(jnp.int32, (128, cols.shape[1]), 0) == at_y, 1.0, 0.0)
    dense = lax.dot_general(
        weights, hot, (((1,), (1,)), ((), ())),
        precision=lax.Precision.HIGHEST, preferred_element_type=F32,
    )
    dense_ref[...] = dense.reshape(dense_ref.shape)


def pick_kernel(owner_ref, got_ref, out_ref, *, which):
    owner = owner_ref[which]
    copies = out_ref.shape[0] // 8
    for n in range(8):
        value = got_ref[n]
        for m in range(1, got_ref.shape[0] // 8):
            value = jnp.where(owner == m, got_ref[8 * m + n], value)
        for m in range(copies):
            out_ref[8 * m + n] = value


def rows(n):
    return pl.ds(8 * n if isinstance(n, int) else pl.multiple_of(8 * n, 8), 8), slice(None)


FX, FY, FZ, MASS = range(4)
HALO = [(FX, 0, 4), (MASS, 0, 4), (FY, 0, 3), (FZ, 0, 3), (FX, 1, 1), (MASS, 1, 1)]
BODY = 27
SENT = BODY + sum(k for _, _, k in HALO)


def fill_body(out, last, tracers_ref, conv_ref):
    for i in range(4):
        for n in range(6):
            out[6 * i + n] = column(tracers_ref, 64 * i, 2 * last + n)
    for n in range(3):
        out[24 + n] = conv_ref[5 * last + n]


def fill_met(out, at, last, met_ref):
    for field, step, k in HALO:
        for n in range(k):
            out[at + n] = met_ref[32 * step + 8 * field + (8 - k) * last + n]
        at += k


def send_body_kernel(tracers_ref, conv_ref, far_ref, mate_ref):
    core = lax.axis_index("core")
    fill_body(far_ref, core, tracers_ref, conv_ref)
    fill_body(mate_ref, 1 - core, tracers_ref, conv_ref)


def send_met_kernel(met_ref, body_ref, far_ref, mate_ref):
    core = lax.axis_index("core")
    fill_met(far_ref, 0, core, met_ref)
    for n in range(BODY):
        mate_ref[n] = body_ref[n]
    fill_met(mate_ref, BODY, 1 - core, met_ref)


def clipped(value, bound):
    return jnp.maximum(jnp.minimum(value, jnp.maximum(bound, 0.0)), jnp.minimum(bound, 0.0))


def edge_offset(before, here, after):
    return clipped(0.5 * here + (1.0 / 12.0) * (before - after), here)


def limited(u, v):
    return clipped(u, v + v), clipped(v, u + u)


def face_factors(flux, near, far):
    size = jnp.abs(flux)
    share = size * jnp.where(flux > 0.0, near, far)
    rest = size * (1.0 - share)
    return rest * (1.0 - share), rest * share


def sweep_y(q, flux, k1, k2, per_mass, open_face):
    def ahead(x):
        return pltpu.roll(x, 127, 1)

    def behind(x):
        return pltpu.roll(x, 1, 1)

    q_next = ahead(q)
    diff = jnp.where(open_face, q_next - q, 0.0)
    u = edge_offset(behind(diff), diff, ahead(diff))
    v = behind(diff - u)
    u, v = limited(u, v)
    forward = flux > 0.0
    transport = (
        flux * jnp.where(forward, q, q_next)
        + k1 * jnp.where(forward, u, ahead(v))
        + k2 * jnp.where(forward, v, ahead(u))
    )
    return q - (transport - behind(transport)) * per_mass


def sweep_z(q, faces, per_mass):
    diff = [q[k + 1] - q[k] for k in range(7)]
    zero = jnp.zeros_like(q[0])
    u, v = [zero] * 8, [zero] * 8
    edge, rest = {}, {}
    for k in range(7):
        slope = diff[k - 1] - diff[k + 1] if 0 < k < 6 else (-diff[1] if k == 0 else diff[5])
        edge[k] = clipped(0.5 * diff[k] + (1.0 / 12.0) * slope, diff[k])
        rest[k + 1] = diff[k] - edge[k]
        if k > 0:
            u[k], v[k] = limited(edge[k], rest[k])
    out, before = [], None
    for k in range(8):
        if k < 7:
            flux, k1, k2 = faces(k)
            forward = flux > 0.0
            sent = (
                flux * jnp.where(forward, q[k], q[k + 1])
                + k1 * jnp.where(forward, u[k], v[k + 1])
                + k2 * jnp.where(forward, v[k], u[k + 1])
            )
            change = sent if before is None else sent - before
            before = sent
        else:
            change = -before
        out.append(q[k] - change * per_mass(k))
    return out


def stage(wide, cells, tables, met_ref, tracers_ref, conv_ref, halos):
    for bulk, got, right in halos:
        if cells is not None:
            for i in range(4):
                for n in range(6):
                    cells[rows(20 * i + 14 * right + n)] = bulk(6 * i + n)
            for n in range(3):
                tables[rows(11 * right + n)] = bulk(24 + n)
        at = 0
        for field, step, k in HALO:
            if (field, step) in wide:
                for n in range(k):
                    wide[field, step][rows((8 + k) * right + n)] = got(at + n)
            at += k
    for x in range(8):
        if cells is not None:
            for i in range(4):
                cells[rows(20 * i + 6 + x)] = column(tracers_ref, 64 * i, x)
            tables[rows(3 + x)] = conv_ref[x]
        for field, step, k in HALO:
            if (field, step) in wide:
                wide[field, step][rows(k + x)] = met_ref[rows(32 * step + 8 * field + x)]


def level(ref, first, k):
    return ref[pl.ds(8 * first + k, 8, stride=8), :]


def advance(count, shift, cell, flux_x, mass, flux_y, flux_z, tables, window, emit, swept, factors, per_mass, lines):
    for n in range(count + 2):
        per_mass[rows(n + 2)] = 1.0 / mass(n)
    for n in range(count + 1):
        flux = flux_x(n)
        k1, k2 = face_factors(flux, per_mass[rows(n + 2)], per_mass[rows(n + 3)])
        factors[0, n], factors[1, n], factors[2, n] = flux, k1, k2

    for i in range(4):
        q, diff, u, v, sent = {}, {}, {}, {}, {}
        for e in range(-3, count + 3):
            q[e] = cell(i, e + 3)
            if e - 1 in q:
                diff[e - 1] = q[e] - q[e - 1]
            if e - 3 in diff:
                u[e - 2] = edge_offset(diff[e - 3], diff[e - 2], diff[e - 1])
                v[e - 1] = diff[e - 2] - u[e - 2]
            j = e - 2
            if j in v:
                u[j], v[j] = limited(u[j], v[j])
            j = e - 3
            if -1 <= j < count:
                flux = factors[0, j + 1]
                forward = flux > 0.0
                sent[j] = (
                    flux * jnp.where(forward, q[j], q[j + 1])
                    + factors[1, j + 1] * jnp.where(forward, u[j], v[j + 1])
                    + factors[2, j + 1] * jnp.where(forward, v[j], u[j + 1])
                )
            if 0 <= j < count:
                swept[rows(8 * i + j + shift)] = q[j] - (sent[j] - sent[j - 1]) * per_mass[rows(j + 3)]

    open_y = lax.broadcasted_iota(jnp.int32, (8, 128), 1) < 127
    substeps = level(tables, window, 0)
    for k in range(8):
        r = level(per_mass, 3 - shift, k)
        fy = jnp.where(open_y, flux_y(k), 0.0)
        y1, y2 = face_factors(fy, r, pltpu.roll(r, 127, 1))
        lines[0, k], lines[1, k], lines[2, k], lines[3, k] = r, fy, y1, y2
        if k > 0:
            fz = flux_z(k - 1)
            z1, z2 = face_factors(fz, r_below, r)
            lines[4, k - 1], lines[5, k - 1], lines[6, k - 1] = fz, z1, z2
            rate = level(tables, window, k)
            lines[7, k] = rate
            lines[8, k] = jnp.where(substeps > 1.5, rate, 0.0)
            lines[9, k] = jnp.where(substeps > 2.5, rate, 0.0)
        r_below = r

    for i in range(4):
        q = [level(swept, 8 * i, k) for k in range(8)]
        q = [sweep_y(q[k], lines[1, k], lines[2, k], lines[3, k], lines[0, k], open_y) for k in range(8)]
        q = sweep_z(q, lambda k: (lines[4, k], lines[5, k], lines[6, k]), lambda k: lines[0, k])
        for m in (7, 8, 9):
            up = [None] + [lines[m, k] for k in range(1, 8)]
            q = [
                (q[k] * (1.0 - up[k + 1]) if k < 7 else q[k]) + (up[k] * q[k - 1] if k > 0 else 0.0)
                for k in range(8)
            ]
        for k in range(8):
            emit(i, k, q[k])


def near_kernel(
    met_ref, tracers_ref, conv_ref, mate_ref, out_ref,
    cells, fx_0, mass_0, fy_0, fz_0, tables, swept, factors, per_mass, lines,
):
    core = lax.axis_index("core")
    wide = {(FX, 0): fx_0, (MASS, 0): mass_0, (FY, 0): fy_0, (FZ, 0): fz_0}
    stage(wide, cells, tables, met_ref, tracers_ref, conv_ref, ((lambda n: mate_ref[1 - core, n], lambda n: mate_ref[1 - core, BODY + n], 1 - core),))
    base = 6 * (1 - core)

    def emit(i, k, q):
        out_ref[pl.ds(64 * i + k, 8, stride=8), :] = q

    advance(
        8, 0, lambda i, n: cells[rows(20 * i + base + n)], lambda n: fx_0[rows(base + n)], lambda n: mass_0[rows(base + n)],
        lambda k: level(fy_0, base, k), lambda k: level(fz_0, base, k), tables, base, emit, swept, factors, per_mass, lines,
    )


def far_kernel(
    met_ref, tracers_ref, conv_ref, mate_ref, bulk_ref, far_ref, near_ref, out_ref,
    cells, fx_0, mass_0, fy_0, fz_0, fx_1, mass_1, tables, state, swept, factors, per_mass, lines,
):
    core = lax.axis_index("core")
    wide = {(FX, 0): fx_0, (MASS, 0): mass_0, (FY, 0): fy_0, (FZ, 0): fz_0}
    far = (lambda n: bulk_ref[n], lambda n: far_ref[n], core)
    mate = (None, lambda n: mate_ref[1 - core, BODY + n], 1 - core)
    stage(wide, cells, tables, met_ref, tracers_ref, conv_ref, (far,))
    stage({(FX, 1): fx_1, (MASS, 1): mass_1}, None, None, met_ref, None, None, (far, mate))
    base, window = 8 * core, 6 * core

    def keep(i, k, q):
        state[pl.ds(8 * (14 * i + window) + k, 8, stride=8), :] = q

    advance(
        6, 2 * core, lambda i, n: cells[rows(20 * i + base + n)], lambda n: fx_0[rows(base + n)], lambda n: mass_0[rows(base + n)],
        lambda k: level(fy_0, window, k), lambda k: level(fz_0, window, k), tables, window, keep, swept, factors, per_mass, lines,
    )
    for i in range(4):
        for n in range(8):
            state[rows(14 * i + 6 * (1 - core) + n)] = near_ref[rows(8 * i + n)]

    def emit(i, k, q):
        out_ref[rows(8 * i + k)] = q

    advance(
        8, 0, lambda i, n: state[rows(14 * i + n)], lambda n: fx_1[rows(n)], lambda n: mass_1[rows(n)],
        lambda k: level(met_ref, 32 + 8 * FY, k), lambda k: level(met_ref, 32 + 8 * FZ, k), tables, 3, emit, swept, factors, per_mass, lines,
    )


def body(tracers, flux_pool, mass_pool, owner, conv_cols, conv_steps, conv_rate):
    packed, owners, dense = call(
        pack_kernel, (shaped(64, 8, 128), shaped(2, 8, 128, dtype=jnp.int32), shaped(8, 8, 128)),
        flux_pool.reshape(384, 128), mass_pool.reshape(128, 128), owner.reshape(1, 2),
        conv_cols, conv_steps, conv_rate.reshape(7, 1, 256), near=False,
    )
    lines = tracers.reshape(256, 128)
    size = lax.axis_size(TILE)
    distant = [(i, (i + 2 * (i % 2) - 1) % size) for i in range(size)]
    body_far, body_mate = call(send_body_kernel, (shaped(BODY, 8, 128), shaped(BODY, 8, 128)), lines, dense)
    dealt = lax.all_to_all(packed, NEAR, 0, 0, tiled=True)
    far_bulk = lax.ppermute(body_far, TILE, distant)
    third = call(functools.partial(pick_kernel, which=0), shaped(24, 8, 128), owners, dealt)
    thirds = lax.all_to_all(third, "za", 0, 0, tiled=True)
    own = call(functools.partial(pick_kernel, which=1), shaped(64, 8, 128), owners, thirds)
    met = lax.all_to_all(own, NEAR, 0, 0, tiled=True)
    to_far, to_mate = call(send_met_kernel, (shaped(SENT - BODY, 8, 128), shaped(SENT, 8, 128)), met, body_mate)
    from_far = lax.ppermute(to_far, TILE, distant)
    from_mate = lax.all_gather(to_mate, "core")

    def columns(n):
        return pltpu.VMEM((8 * n, 128), F32)

    met = met.reshape(512, 128)
    arrays = [columns(80)] + [columns(8 + 2 * k) for _, _, k in HALO[:4]]
    work = [columns(32), pltpu.VMEM((3, 9, 8, 128), F32), columns(12), pltpu.VMEM((10, 8, 8, 128), F32)]
    ahead = call(
        near_kernel, shaped(256, 128), met, lines, dense, from_mate,
        scratch=arrays + [columns(14)] + work, flops=3000000,
    )
    out = call(
        far_kernel, jax.ShapeDtypeStruct((256, 128), F32), met, lines, dense, from_mate, far_bulk, from_far, ahead,
        scratch=arrays + [columns(10)] * 2 + [columns(14), columns(56)] + work, flops=5000000,
    )
    return out.reshape(tracers.shape)


def solution(mesh):
    split = Mesh(mesh.devices.reshape(2, 8, 2, 2, 3, 4), TILE + TRC)
    in_specs = (
        P(TRC, None, TILE, None),
        P(TRC, None, None, None, TILE, None),
        P(TRC, None, None, TILE, None),
        P(None, TILE),
        P(TILE, None),
        P(TILE, None),
        P(TILE, None, None),
    )
    out_specs = P(TRC, None, TILE, None)
    return jax.shard_map(body, mesh=split, in_specs=in_specs, out_specs=out_specs, check_vma=False)
```

```python
import functools

import jax
import jax.numpy as jnp
from jax import lax
from jax.experimental import pallas as pl
from jax.experimental.pallas import tpu as pltpu
from jax.sharding import Mesh, PartitionSpec as P

TILE = ("x_hi", "y", "core")
TRC = ("x_lo", "za", "zb")
NEAR = ("x_lo", "zb")
VM = pl.BlockSpec(memory_space=pltpu.VMEM)
F32 = jnp.float32


def shaped(*shape, dtype=F32):
    return pltpu.VMEM(shape, dtype)


def call(kernel, outs, *args, scratch=(), flops=20000, near=True):
    size = sum(4 * a.size for a in args)
    return pl.pallas_call(
        kernel,
        out_shape=outs,
        in_specs=[VM] * len(args),
        out_specs=jax.tree.map(lambda _: VM, outs),
        scratch_shapes=list(scratch),
        cost_estimate=pl.CostEstimate(flops=flops, bytes_accessed=size, transcendentals=0),
    )(*[pltpu.with_memory_space_constraint(a, pltpu.VMEM) if near else a for a in args])


def column(ref, first, x):
    return ref[pl.ds(first + x, 8, stride=8), :]


def pack_kernel(flux_ref, mass_ref, owner_ref, out_ref, owner_out):
    for s in range(2):
        for x in range(8):
            for f in range(3):
                out_ref[32 * s + 8 * f + x] = column(flux_ref, (s * 3 + f) * 64, x)
            out_ref[32 * s + 24 + x] = column(mass_ref, s * 64, x)
    first = lax.axis_index("x_lo") == 0
    owner = jnp.broadcast_to(jnp.where(first, owner_ref[0:1, 0:1], owner_ref[0:1, 1:2]), (8, 128))
    owner_out[0] = 4 * (owner // 12) + owner % 4
    owner_out[1] = (owner % 12) // 4


def pick_kernel(owner_ref, got_ref, out_ref, *, which):
    owner = owner_ref[which]
    copies = out_ref.shape[0] // 8
    for n in range(8):
        value = got_ref[n]
        for m in range(1, got_ref.shape[0] // 8):
            value = jnp.where(owner == m, got_ref[8 * m + n], value)
        for m in range(copies):
            out_ref[8 * m + n] = value


def rows(n):
    return pl.ds(8 * n if isinstance(n, int) else pl.multiple_of(8 * n, 8), 8), slice(None)


FX, FY, FZ, MASS = range(4)
HALO = [(FX, 0, 4), (MASS, 0, 4), (FY, 0, 3), (FZ, 0, 3), (FX, 1, 1), (MASS, 1, 1)]
BODY = 27
SENT = BODY + sum(k for _, _, k in HALO)


def fill_body(out, last, tracers_ref, conv_ref):
    for i in range(4):
        for n in range(6):
            out[6 * i + n] = column(tracers_ref, 64 * i, 2 * last + n)
    for n in range(3):
        out[24 + n] = conv_ref[5 * last + n]


def fill_met(out, at, last, met_ref):
    for field, step, k in HALO:
        for n in range(k):
            out[at + n] = met_ref[32 * step + 8 * field + (8 - k) * last + n]
        at += k


def send_body_kernel(tracers_ref, cols_ref, steps_ref, rate_ref, far_ref, mate_ref, dense_ref):
    cols = cols_ref[...]
    at_x, at_y = cols // 128, cols % 128
    values = jnp.concatenate([steps_ref[...].astype(F32), rate_ref[:, 0, :]], axis=0)
    weights = jnp.concatenate([jnp.where(at_x == x, values, 0.0) for x in range(8)], axis=0)
    hot = jnp.where(lax.broadcasted_iota(jnp.int32, (128, cols.shape[1]), 0) == at_y, 1.0, 0.0)
    dense = lax.dot_general(
        weights, hot, (((1,), (1,)), ((), ())),
        precision=lax.Precision.HIGHEST, preferred_element_type=F32,
    )
    dense_ref[...] = dense.reshape(dense_ref.shape)
    core = lax.axis_index("core")
    fill_body(far_ref, core, tracers_ref, dense_ref)
    fill_body(mate_ref, 1 - core, tracers_ref, dense_ref)


def send_met_kernel(met_ref, body_ref, far_ref, mate_ref):
    core = lax.axis_index("core")
    fill_met(far_ref, 0, core, met_ref)
    for n in range(BODY):
        mate_ref[n] = body_ref[n]
    fill_met(mate_ref, BODY, 1 - core, met_ref)


def clipped(value, bound):
    return jnp.maximum(jnp.minimum(value, jnp.maximum(bound, 0.0)), jnp.minimum(bound, 0.0))


def edge_offset(before, here, after):
    return clipped(0.5 * here + (1.0 / 12.0) * (before - after), here)


def limited(u, v):
    return clipped(u, v + v), clipped(v, u + u)


def face_factors(flux, near, far):
    size = jnp.abs(flux)
    share = size * jnp.where(flux > 0.0, near, far)
    rest = size * (1.0 - share)
    return rest * (1.0 - share), rest * share


def sweep_y(q, flux, k1, k2, per_mass, open_face):
    def ahead(x):
        return pltpu.roll(x, 127, 1)

    def behind(x):
        return pltpu.roll(x, 1, 1)

    q_next = ahead(q)
    diff = jnp.where(open_face, q_next - q, 0.0)
    u = edge_offset(behind(diff), diff, ahead(diff))
    v = behind(diff - u)
    u, v = limited(u, v)
    forward = flux > 0.0
    transport = (
        flux * jnp.where(forward, q, q_next)
        + k1 * jnp.where(forward, u, ahead(v))
        + k2 * jnp.where(forward, v, ahead(u))
    )
    return q - (transport - behind(transport)) * per_mass


def sweep_z(q, faces, per_mass):
    diff = [q[k + 1] - q[k] for k in range(7)]
    zero = jnp.zeros_like(q[0])
    u, v = [zero] * 8, [zero] * 8
    edge, rest = {}, {}
    for k in range(7):
        slope = diff[k - 1] - diff[k + 1] if 0 < k < 6 else (-diff[1] if k == 0 else diff[5])
        edge[k] = clipped(0.5 * diff[k] + (1.0 / 12.0) * slope, diff[k])
        rest[k + 1] = diff[k] - edge[k]
        if k > 0:
            u[k], v[k] = limited(edge[k], rest[k])
    out, before = [], None
    for k in range(8):
        if k < 7:
            flux, k1, k2 = faces(k)
            forward = flux > 0.0
            sent = (
                flux * jnp.where(forward, q[k], q[k + 1])
                + k1 * jnp.where(forward, u[k], v[k + 1])
                + k2 * jnp.where(forward, v[k], u[k + 1])
            )
            change = sent if before is None else sent - before
            before = sent
        else:
            change = -before
        out.append(q[k] - change * per_mass(k))
    return out


def stage(wide, cells, tables, met_ref, tracers_ref, conv_ref, halos):
    for bulk, got, right in halos:
        if cells is not None:
            for i in range(4):
                for n in range(6):
                    cells[rows(20 * i + 14 * right + n)] = bulk(6 * i + n)
            for n in range(3):
                tables[rows(11 * right + n)] = bulk(24 + n)
        at = 0
        for field, step, k in HALO:
            if (field, step) in wide:
                for n in range(k):
                    wide[field, step][rows((8 + k) * right + n)] = got(at + n)
            at += k
    for x in range(8):
        if cells is not None:
            for i in range(4):
                cells[rows(20 * i + 6 + x)] = column(tracers_ref, 64 * i, x)
            tables[rows(3 + x)] = conv_ref[x]
        for field, step, k in HALO:
            if (field, step) in wide:
                wide[field, step][rows(k + x)] = met_ref[rows(32 * step + 8 * field + x)]


def level(ref, first, k):
    return ref[pl.ds(8 * first + k, 8, stride=8), :]


def advance(count, shift, cell, flux_x, mass, flux_y, flux_z, tables, window, emit, swept, factors, per_mass, lines):
    for n in range(count + 2):
        per_mass[rows(n + 2)] = 1.0 / mass(n)
    for n in range(count + 1):
        flux = flux_x(n)
        k1, k2 = face_factors(flux, per_mass[rows(n + 2)], per_mass[rows(n + 3)])
        factors[0, n], factors[1, n], factors[2, n] = flux, k1, k2

    for i in range(4):
        q, diff, u, v, sent = {}, {}, {}, {}, {}
        for e in range(-3, count + 3):
            q[e] = cell(i, e + 3)
            if e - 1 in q:
                diff[e - 1] = q[e] - q[e - 1]
            if e - 3 in diff:
                u[e - 2] = edge_offset(diff[e - 3], diff[e - 2], diff[e - 1])
                v[e - 1] = diff[e - 2] - u[e - 2]
            j = e - 2
            if j in v:
                u[j], v[j] = limited(u[j], v[j])
            j = e - 3
            if -1 <= j < count:
                flux = factors[0, j + 1]
                forward = flux > 0.0
                sent[j] = (
                    flux * jnp.where(forward, q[j], q[j + 1])
                    + factors[1, j + 1] * jnp.where(forward, u[j], v[j + 1])
                    + factors[2, j + 1] * jnp.where(forward, v[j], u[j + 1])
                )
            if 0 <= j < count:
                swept[rows(8 * i + j + shift)] = q[j] - (sent[j] - sent[j - 1]) * per_mass[rows(j + 3)]

    open_y = lax.broadcasted_iota(jnp.int32, (8, 128), 1) < 127
    substeps = level(tables, window, 0)
    for k in range(8):
        r = level(per_mass, 3 - shift, k)
        fy = jnp.where(open_y, flux_y(k), 0.0)
        y1, y2 = face_factors(fy, r, pltpu.roll(r, 127, 1))
        lines[0, k], lines[1, k], lines[2, k], lines[3, k] = r, fy, y1, y2
        if k > 0:
            fz = flux_z(k - 1)
            z1, z2 = face_factors(fz, r_below, r)
            lines[4, k - 1], lines[5, k - 1], lines[6, k - 1] = fz, z1, z2
            rate = level(tables, window, k)
            lines[7, k] = rate
            lines[8, k] = jnp.where(substeps > 1.5, rate, 0.0)
            lines[9, k] = jnp.where(substeps > 2.5, rate, 0.0)
        r_below = r

    for i in range(4):
        q = [level(swept, 8 * i, k) for k in range(8)]
        q = [sweep_y(q[k], lines[1, k], lines[2, k], lines[3, k], lines[0, k], open_y) for k in range(8)]
        q = sweep_z(q, lambda k: (lines[4, k], lines[5, k], lines[6, k]), lambda k: lines[0, k])
        for m in (7, 8, 9):
            up = [None] + [lines[m, k] for k in range(1, 8)]
            q = [
                (q[k] * (1.0 - up[k + 1]) if k < 7 else q[k]) + (up[k] * q[k - 1] if k > 0 else 0.0)
                for k in range(8)
            ]
        for k in range(8):
            emit(i, k, q[k])


def near_kernel(
    met_ref, tracers_ref, conv_ref, mate_ref, out_ref,
    cells, fx_0, mass_0, fy_0, fz_0, tables, swept, factors, per_mass, lines,
):
    core = lax.axis_index("core")
    wide = {(FX, 0): fx_0, (MASS, 0): mass_0, (FY, 0): fy_0, (FZ, 0): fz_0}
    stage(wide, cells, tables, met_ref, tracers_ref, conv_ref, ((lambda n: mate_ref[1 - core, n], lambda n: mate_ref[1 - core, BODY + n], 1 - core),))
    base = 6 * (1 - core)

    def emit(i, k, q):
        out_ref[pl.ds(64 * i + k, 8, stride=8), :] = q

    advance(
        8, 0, lambda i, n: cells[rows(20 * i + base + n)], lambda n: fx_0[rows(base + n)], lambda n: mass_0[rows(base + n)],
        lambda k: level(fy_0, base, k), lambda k: level(fz_0, base, k), tables, base, emit, swept, factors, per_mass, lines,
    )


def far_kernel(
    met_ref, tracers_ref, conv_ref, mate_ref, bulk_ref, far_ref, near_ref, out_ref,
    cells, fx_0, mass_0, fy_0, fz_0, fx_1, mass_1, tables, state, swept, factors, per_mass, lines,
):
    core = lax.axis_index("core")
    wide = {(FX, 0): fx_0, (MASS, 0): mass_0, (FY, 0): fy_0, (FZ, 0): fz_0}
    far = (lambda n: bulk_ref[n], lambda n: far_ref[n], core)
    mate = (None, lambda n: mate_ref[1 - core, BODY + n], 1 - core)
    stage(wide, cells, tables, met_ref, tracers_ref, conv_ref, (far,))
    stage({(FX, 1): fx_1, (MASS, 1): mass_1}, None, None, met_ref, None, None, (far, mate))
    base, window = 8 * core, 6 * core

    def keep(i, k, q):
        state[pl.ds(8 * (14 * i + window) + k, 8, stride=8), :] = q

    advance(
        6, 2 * core, lambda i, n: cells[rows(20 * i + base + n)], lambda n: fx_0[rows(base + n)], lambda n: mass_0[rows(base + n)],
        lambda k: level(fy_0, window, k), lambda k: level(fz_0, window, k), tables, window, keep, swept, factors, per_mass, lines,
    )
    for i in range(4):
        for n in range(8):
            state[rows(14 * i + 6 * (1 - core) + n)] = near_ref[rows(8 * i + n)]

    def emit(i, k, q):
        out_ref[rows(8 * i + k)] = q

    advance(
        8, 0, lambda i, n: state[rows(14 * i + n)], lambda n: fx_1[rows(n)], lambda n: mass_1[rows(n)],
        lambda k: level(met_ref, 32 + 8 * FY, k), lambda k: level(met_ref, 32 + 8 * FZ, k), tables, 3, emit, swept, factors, per_mass, lines,
    )


def body(tracers, flux_pool, mass_pool, owner, conv_cols, conv_steps, conv_rate):
    packed, owners = call(
        pack_kernel, (shaped(64, 8, 128), shaped(2, 8, 128, dtype=jnp.int32)),
        flux_pool.reshape(384, 128), mass_pool.reshape(128, 128), owner.reshape(1, 2), near=False,
    )
    lines = tracers.reshape(256, 128)
    size = lax.axis_size(TILE)
    distant = [(i, (i + 2 * (i % 2) - 1) % size) for i in range(size)]
    body_far, body_mate, dense = call(
        send_body_kernel, (shaped(BODY, 8, 128), shaped(BODY, 8, 128), shaped(8, 8, 128)),
        lines, conv_cols, conv_steps, conv_rate.reshape(7, 1, 256),
    )
    dealt = lax.all_to_all(packed, NEAR, 0, 0, tiled=True)
    far_bulk = lax.ppermute(body_far, TILE, distant)
    third = call(functools.partial(pick_kernel, which=0), shaped(24, 8, 128), owners, dealt)
    thirds = lax.all_to_all(third, "za", 0, 0, tiled=True)
    own = call(functools.partial(pick_kernel, which=1), shaped(64, 8, 128), owners, thirds)
    met = lax.all_to_all(own, NEAR, 0, 0, tiled=True)
    to_far, to_mate = call(send_met_kernel, (shaped(SENT - BODY, 8, 128), shaped(SENT, 8, 128)), met, body_mate)
    from_far = lax.ppermute(to_far, TILE, distant)
    from_mate = lax.all_gather(to_mate, "core")

    def columns(n):
        return pltpu.VMEM((8 * n, 128), F32)

    met = met.reshape(512, 128)
    arrays = [columns(80)] + [columns(8 + 2 * k) for _, _, k in HALO[:4]]
    work = [columns(32), pltpu.VMEM((3, 9, 8, 128), F32), columns(12), pltpu.VMEM((10, 8, 8, 128), F32)]
    ahead = call(
        near_kernel, shaped(256, 128), met, lines, dense, from_mate,
        scratch=arrays + [columns(14)] + work, flops=3000000,
    )
    out = call(
        far_kernel, jax.ShapeDtypeStruct((256, 128), F32), met, lines, dense, from_mate, far_bulk, from_far, ahead,
        scratch=arrays + [columns(10)] * 2 + [columns(14), columns(56)] + work, flops=5000000,
    )
    return out.reshape(tracers.shape)


def solution(mesh):
    split = Mesh(mesh.devices.reshape(2, 8, 2, 2, 3, 4), TILE + TRC)
    in_specs = (
        P(TRC, None, TILE, None),
        P(TRC, None, None, None, TILE, None),
        P(TRC, None, None, TILE, None),
        P(None, TILE),
        P(TILE, None),
        P(TILE, None),
        P(TILE, None, None),
    )
    out_specs = P(TRC, None, TILE, None)
    return jax.shard_map(body, mesh=split, in_specs=in_specs, out_specs=out_specs, check_vma=False)
```
